128 devices in a mesh: gx: 16 (over x, y), gy: 4 (over z), gz: 2 (over core).
Axes of the slice: x: 4, y: 4, z: 4, core: 2. Of those that a mesh axis runs over, the one named last changes fastest.
Arguments:
- conserved: float32 [14, 128, 256, 512], P(None, 'gx', 'gy', 'gz')
- char_left: float32 [14, 14], replicated
- char_right: float32 [14, 14], replicated
- shock_list: int32 [16, 4, 2, 128], P('gx', 'gy', 'gz'), may hold values from 0 to 511, as said below
- shock_count: int32 [16, 4, 2], P('gx', 'gy', 'gz'), may hold values from 32 to 128, as said below
Outputs:
- advanced: float32 [14, 128, 256, 512], P(None, 'gx', 'gy', 'gz')
The draws below stay inside these ranges and needn't reach their ends.
Inputs may be any that keep to these rules, and one draw needn't show every extreme that they name: `shock_list`: the entries of one device's list are distinct local pencil indices; only the first shock_count of them are shocked pencils. `shock_count`: in every column of devices along gx (fixed gy and gz index) one device has 128 shocked pencils and every other device has 32, so a column holds 608 in all.
All inputs are finite; a program needn't handle non-finite values.
Results may differ from the reference program's by a relative error of at most 0.00005.
Values sent between devices are 32-bit elements; how exact they have to be, the bound alone decides.
A program may use at most 192 MiB of HBM per device.

```python
import math
import jax
import jax.numpy as jnp
from jax import lax

SPECIES = 9
VARIABLES = 14
CX = 8
CY = 64
CZ = 256
SHOCK_MAX = 128
NX = 128
NY = 256
NZ = 512
N_GX = 16
N_GY = 4
N_GZ = 2


def draw_conserved(key, part):
    grid_shape = (NX, NY, NZ)
    subkeys = jax.random.split(key, 4)
    species = jnp.exp(jax.random.uniform(subkeys[0], (SPECIES,) + grid_shape, jnp.float32, math.log(0.05), math.log(0.5)))
    momenta = jnp.clip(jax.random.normal(subkeys[1], (3,) + grid_shape, jnp.float32), -3.0, 3.0)
    energy = jax.random.uniform(subkeys[2], (1,) + grid_shape, jnp.float32, 2.5, 5.0)
    vibration = jax.random.uniform(subkeys[3], (1,) + grid_shape, jnp.float32, 0.1, 0.8)
    return jnp.concatenate([species, momenta, energy, vibration], axis=0)


def basis_matrix(key, salt):
    inner_key = jax.random.fold_in(key, salt)
    noise = jax.random.normal(inner_key, (VARIABLES, VARIABLES), jnp.float32)
    return jnp.eye(VARIABLES, dtype=jnp.float32) + 0.3 / math.sqrt(VARIABLES) * noise


def draw_char_left(key, part):
    return basis_matrix(key, 31)


def draw_char_right(key, part):
    return basis_matrix(key, 57)


def draw_shock_list(key, part):
    pencil_total = CX * CY
    scores = jax.random.randint(jax.random.fold_in(key, 11), (N_GX, N_GY, N_GZ, pencil_total), 0, 1 << 16)
    distinct = scores * pencil_total + jnp.arange(pencil_total, dtype=jnp.int32)
    ordering = jnp.argsort(distinct, axis=-1)
    return ordering[..., :SHOCK_MAX].astype(jnp.int32)


def draw_shock_count(key, part):
    front = jax.random.randint(jax.random.fold_in(key, 23), (1, N_GY, N_GZ), 0, N_GX)
    column = jnp.arange(N_GX, dtype=jnp.int32)[:, None, None]
    return jnp.where(column == front, SHOCK_MAX, SHOCK_MAX // 4).astype(jnp.int32)


def setup_inputs(seed: int = 0) -> dict:
    arg_keys = jax.random.split(jax.random.key(seed), 6)
    conserved = draw_conserved(jax.random.fold_in(arg_keys[5], 71), 0)
    char_left = draw_char_left(jax.random.fold_in(arg_keys[5], 71), 0)
    char_right = draw_char_right(jax.random.fold_in(arg_keys[5], 71), 0)
    shock_list = draw_shock_list(jax.random.fold_in(arg_keys[5], 71), 0)
    shock_count = draw_shock_count(jax.random.fold_in(arg_keys[5], 71), 0)
    return {"conserved": conserved, "char_left": char_left, "char_right": char_right, "shock_list": shock_list, "shock_count": shock_count}


gas_excess = 0.4
time_step = 0.2
weno_epsilon = 1e-6


def directed_flux(values_in, normal):
    density = jnp.sum(values_in[:SPECIES], axis=0)
    inverse = 1.0 / density
    velocity = values_in[SPECIES + normal] * inverse
    momenta = values_in[SPECIES:SPECIES + 3]
    kinetic = 0.5 * jnp.sum(momenta * momenta, axis=0) * inverse
    pressure = gas_excess * (values_in[SPECIES + 3] - values_in[SPECIES + 4] - kinetic)
    result = values_in * velocity[None]
    result = result.at[SPECIES + normal].add(pressure)
    result = result.at[SPECIES + 3].add(pressure * velocity)
    return result


def central_difference(values_in, dimension, length_cells):
    def shifted(begin_at):
        return lax.slice_in_dim(values_in, begin_at, begin_at + length_cells, axis=dimension)
    return (45.0 * (shifted(4) - shifted(2)) - 9.0 * (shifted(5) - shifted(1)) + (shifted(6) - shifted(0))) / 60.0


def upwind_value(first_cell, second_cell, middle, fourth_cell, fifth_cell):
    stencil_zero = (2.0 * first_cell - 7.0 * second_cell + 11.0 * middle) / 6.0
    stencil_one = (-second_cell + 5.0 * middle + 2.0 * fourth_cell) / 6.0
    stencil_two = (2.0 * middle + 5.0 * fourth_cell - fifth_cell) / 6.0
    smooth_zero = 13.0 / 12.0 * (first_cell - 2.0 * second_cell + middle) ** 2 + 0.25 * (first_cell - 4.0 * second_cell + 3.0 * middle) ** 2
    smooth_one = 13.0 / 12.0 * (second_cell - 2.0 * middle + fourth_cell) ** 2 + 0.25 * (second_cell - fourth_cell) ** 2
    smooth_two = 13.0 / 12.0 * (middle - 2.0 * fourth_cell + fifth_cell) ** 2 + 0.25 * (3.0 * middle - 4.0 * fourth_cell + fifth_cell) ** 2
    weight_zero = 0.1 / (weno_epsilon + smooth_zero) ** 2
    weight_one = 0.6 / (weno_epsilon + smooth_one) ** 2
    weight_two = 0.3 / (weno_epsilon + smooth_two) ** 2
    return (weight_zero * stencil_zero + weight_one * stencil_one + weight_two * stencil_two) / (weight_zero + weight_one + weight_two)


def weno_divergence(pencils, char_left, char_right):
    fluxes = directed_flux(pencils, 2)
    density = jnp.sum(pencils[:SPECIES], axis=0)
    wave_speed = jnp.max(jnp.abs(pencils[SPECIES + 2] / density), axis=-1) + 1.0
    outward = 0.5 * (fluxes + wave_speed[None, :, None] * pencils)
    inward = 0.5 * (fluxes - wave_speed[None, :, None] * pencils)
    char_out = jnp.einsum("ij,jpk->ipk", char_left, outward, precision=lax.Precision.HIGHEST)
    char_in = jnp.einsum("ij,jpk->ipk", char_left, inward, precision=lax.Precision.HIGHEST)
    face_count = pencils.shape[-1] - 5

    def window(values_in, begin_at):
        return values_in[..., begin_at:begin_at + face_count]

    summed = upwind_value(window(char_out, 0), window(char_out, 1), window(char_out, 2), window(char_out, 3), window(char_out, 4))
    summed = summed + upwind_value(window(char_in, 5), window(char_in, 4), window(char_in, 3), window(char_in, 2), window(char_in, 1))
    face_values = jnp.einsum("ij,jpk->ipk", char_right, summed, precision=lax.Precision.HIGHEST)
    return face_values[..., 1:] - face_values[..., :-1]


def reference(conserved, char_left, char_right, shock_list, shock_count):
    def plane_terms(x_plane):
        along_y = jnp.concatenate([x_plane[:, -3:], x_plane, x_plane[:, :3]], axis=1)
        along_z = jnp.concatenate([x_plane[:, :, -3:], x_plane, x_plane[:, :, :3]], axis=2)
        y_term = central_difference(directed_flux(along_y, 1), 1, NY)
        z_term = central_difference(directed_flux(along_z, 2), 2, NZ)

        def arrange(term):
            return jnp.transpose(term.reshape(VARIABLES, NY, N_GZ, CZ), (1, 2, 0, 3))
        return arrange(y_term), arrange(z_term)

    y_all, z_all = lax.map(plane_terms, jnp.moveaxis(conserved, 1, 0))
    block_x = jnp.arange(N_GX, dtype=jnp.int32)[:, None, None, None]
    block_y = jnp.arange(N_GY, dtype=jnp.int32)[None, :, None, None]
    block_z = jnp.arange(N_GZ, dtype=jnp.int32)[None, None, :, None]
    slot_index = jnp.arange(SHOCK_MAX, dtype=jnp.int32)[None, None, None, :]
    in_list = slot_index < shock_count[..., None]
    pencil_x = (block_x * CX + shock_list // CY).astype(jnp.int32)
    pencil_y = (block_y * CY + shock_list % CY).astype(jnp.int32)
    pencil_z = (block_z + 0 * shock_list).astype(jnp.int32)
    target_x = jnp.where(in_list, pencil_x, NX).reshape(-1).astype(jnp.int32)
    pencil_x = pencil_x.reshape(-1)
    pencil_y = pencil_y.reshape(-1)
    pencil_z = pencil_z.reshape(-1)
    offsets = jnp.arange(-3, CZ + 3, dtype=jnp.int32)
    z_cells = ((pencil_z[:, None] * CZ + offsets[None, :]) % NZ).astype(jnp.int32)
    pencils = conserved[:, pencil_x[:, None], pencil_y[:, None], z_cells]
    weno_terms = weno_divergence(pencils, char_left, char_right)
    z_all = z_all.at[target_x, pencil_y, pencil_z].set(jnp.transpose(weno_terms, (1, 0, 2)), mode="drop")
    combined = jnp.transpose(y_all + z_all, (3, 0, 1, 2, 4)).reshape(VARIABLES, NX, NY, NZ)
    return conserved - time_step * combined
```

```python
import functools

import jax
import jax.numpy as jnp
import numpy as np
from jax import lax
from jax.experimental import pallas as pl
from jax.experimental.pallas import tpu as pltpu
from jax.sharding import PartitionSpec as P

SPECIES = 9
VARIABLES = 14
CX, CY, CZ = 8, 64, 256
ROWS = CX * CY
PENCILS = 128
GROUP = 16
EPS = 0.75e-6
SCALE = 0.2 / 60.0

F32 = jnp.float32
BF16 = jnp.bfloat16
VMEM = pl.BlockSpec(memory_space=pltpu.VMEM)
SMEM = pl.BlockSpec(memory_space=pltpu.SMEM)
ANY = pl.BlockSpec(memory_space=pl.ANY)


def lanes(shape):
    return lax.broadcasted_iota(jnp.int32, shape, len(shape) - 1)


def split(values):
    high = values.astype(BF16)
    low = (values - high.astype(F32)).astype(BF16)
    return high, low


def dot(left, right):
    return jnp.dot(left, right, preferred_element_type=F32)


def pack_body(list_ref, u_hbm, pencil_out, up_out, down_out, zpack_out, u_ref, sems):
    copies = []
    for x in range(CX):
        for t in range(2):
            copy = pltpu.make_async_copy(
                u_hbm.at[:, x, :, pl.ds(128 * t, 128)],
                u_ref.at[t, :, x],
                sems.at[x, t],
            )
            copy.start()
            copies.append(copy)
    lane = lanes((CY, 128))
    for x in range(CX):
        copies[2 * x].wait()
        copies[2 * x + 1].wait()

        def edge(v, carry, x=x):
            ends = jnp.where(lane < 64, u_ref[0, v, x], u_ref[1, v, x])
            ends = pltpu.roll(ends, 16 * x + 3, 1)
            if x == 0:
                zpack_out[v] = ends
            else:
                zpack_out[v] = jnp.where(lane < 16 * x, zpack_out[v], ends)
            for t in range(2):
                down_out[t, v, 3 * x : 3 * x + 3, :] = u_ref[t, v, x, 0:3, :]
                up_out[t, v, 3 * x : 3 * x + 3, :] = u_ref[t, v, x, CY - 3 : CY, :]
            return carry

        lax.fori_loop(0, VARIABLES, edge, 0, unroll=2)
    flat = u_ref.reshape(2, VARIABLES * ROWS, 128)
    packed = pencil_out.reshape(2, VARIABLES * PENCILS, 128)

    def gather(p, carry):
        row = list_ref[p]
        for t in range(2):
            for v in range(VARIABLES):
                packed[t, pl.ds(p + v * PENCILS, 1), :] = flat[t, pl.ds(row + v * ROWS, 1), :]
        return carry

    lax.fori_loop(0, PENCILS, gather, 0, unroll=2)


def pack(conserved, shocked):
    return pl.pallas_call(
        pack_body,
        out_shape=(
            jax.ShapeDtypeStruct((2, VARIABLES, PENCILS, 128), F32),
            jax.ShapeDtypeStruct((2, VARIABLES, 3 * CX, 128), F32),
            jax.ShapeDtypeStruct((2, VARIABLES, 3 * CX, 128), F32),
            jax.ShapeDtypeStruct((VARIABLES, CY, 128), F32),
        ),
        in_specs=[SMEM, ANY],
        out_specs=(VMEM, VMEM, VMEM, VMEM),
        scratch_shapes=[
            pltpu.VMEM((2, VARIABLES, CX, CY, 128), F32),
            pltpu.SemaphoreType.DMA((CX, 2)),
        ],
        name="pack",
    )(shocked, conserved)


CELLS = 288
FACES = 288
TILES = 33


def reciprocal(values):
    guess = pl.reciprocal(values, approx=True)
    return guess * (2.0 - values * guess)


def correction(a, b, c, d, fast):
    zero = a * a + b * (2.5 * b - 2.75 * a) + EPS
    one = b * b + c * (c - 1.25 * b) + EPS
    two = d * d + c * (2.5 * c - 2.75 * d) + EPS
    first = b * (5.0 / 6.0) - a * (1.0 / 3.0)
    second = b * (1.0 / 6.0) + c * (1.0 / 3.0)
    third = c * (2.0 / 3.0) - d * (1.0 / 6.0)
    if fast:
        p12, p02, p01 = one * two, zero * two, zero * one
        w0 = p12 * p12
        w1 = 6.0 * (p02 * p02)
        w2 = 3.0 * (p01 * p01)
        return (w0 * first + w1 * second + w2 * third) * reciprocal(w0 + w1 + w2)
    w0 = 1.0 / (zero * zero)
    w1 = 6.0 / (one * one)
    w2 = 3.0 / (two * two)
    return (w0 * first + w1 * second + w2 * third) / (w0 + w1 + w2)


def weno_body(
    list_ref, columns_ref, where_ref,
    left_ref, right_ref, pencil_ref, halo_ref,
    out_ref,
    cells, gathered, velocity_ref, pressure_ref,
    proj, plus_ref, minus_ref, dplus_ref, dminus_ref, sums, kl1, kl2, kr1, kr2,
):
    size = VARIABLES * GROUP
    r = lax.broadcasted_iota(jnp.int32, (size, size), 0)
    c = lax.broadcasted_iota(jnp.int32, (size, size), 1)
    spread = (
        lax.broadcasted_iota(jnp.int32, (size, VARIABLES), 0) // GROUP
        == lax.broadcasted_iota(jnp.int32, (size, VARIABLES), 1)
    ).astype(F32)
    gatherer = (
        lax.broadcasted_iota(jnp.int32, (VARIABLES, size), 1) // GROUP
        == lax.broadcasted_iota(jnp.int32, (VARIABLES, size), 0)
    ).astype(F32)
    same = (r & (GROUP - 1)) == (c & (GROUP - 1))
    for matrix, scale, high_ref, low_ref in ((left_ref, 0.5, kl1, kl2), (right_ref, 60.0, kr1, kr2)):
        wide = jnp.dot(
            spread,
            jnp.dot(
                scale * matrix[...], gatherer,
                precision=lax.Precision.HIGHEST, preferred_element_type=F32,
            ),
            precision=lax.Precision.HIGHEST, preferred_element_type=F32,
        )
        high, low = split(jnp.where(same, wide, 0.0))
        high_ref[...] = high
        low_ref[...] = low

    halo_rows = halo_ref.reshape(VARIABLES * CY, 128)
    gathered_rows = gathered.reshape(VARIABLES * PENCILS, 128)

    def fetch(p, carry):
        y = list_ref[p] % CY
        for v in range(VARIABLES):
            gathered_rows[pl.ds(p + v * PENCILS, 1), :] = halo_rows[pl.ds(y + v * CY, 1), :]
        return carry

    lax.fori_loop(0, PENCILS, fetch, 0, unroll=2)
    own_x = jnp.broadcast_to(where_ref[...] // CY, (16, 128))

    def turn(v, carry):
        for t in range(2):
            cells[v, 8 + 128 * t : 136 + 128 * t, :] = pencil_ref[t, v].T
        ends = gathered[v].T
        beside = ends[0:16]
        for x in range(1, CX):
            beside = jnp.where(own_x == x, ends[16 * x : 16 * x + 16], beside)
        cells[v, 0:5, :] = beside[0:5]
        cells[v, 5:8, :] = beside[0:3]
        cells[v, 264:267, :] = beside[3:6]
        for at in (267, 272, 277, 282):
            cells[v, at : at + 5, :] = beside[0:5]
        cells[v, 287:288, :] = beside[0:1]
        return carry

    lax.fori_loop(0, VARIABLES, turn, 0)

    def wave(i, carry):
        peak, top = carry
        rows = pl.ds(pl.multiple_of(8 * i, 8), 8)
        values = [cells[v, rows, :] for v in range(VARIABLES)]
        density = values[0]
        for v in range(1, SPECIES):
            density = density + values[v]
        inverse = 1.0 / density
        velocity = values[11] * inverse
        squares = values[9] * values[9] + values[10] * values[10] + values[11] * values[11]
        pressure = 0.4 * (values[12] - values[13] - 0.5 * squares * inverse)
        velocity_ref[rows, :] = velocity
        pressure_ref[rows, :] = pressure
        for value in values + [pressure]:
            top = jnp.maximum(top, jnp.abs(value))
        return jnp.maximum(peak, jnp.abs(velocity)), top

    zero = jnp.zeros((8, 128), F32)
    peak, top = lax.fori_loop(0, CELLS // 8, wave, (zero, zero), unroll=2)
    speed = jnp.broadcast_to(jnp.max(peak, axis=0, keepdims=True) + 1.0, (8, 128))
    largest = jnp.max(top)
    bound = jnp.max(jnp.sum(jnp.abs(left_ref[...]), axis=1, keepdims=True))
    limit = 2.0 * bound * largest * (1.0 + 2.0 * jnp.max(speed))
    safe = limit < 2000.0

    def project(high_ref, low_ref, source, target):
        def chunk(i, carry):
            first = pl.ds(pl.multiple_of(32 * i, 16), 16)
            second = pl.ds(pl.multiple_of(32 * i + 16, 16), 16)
            values = jnp.concatenate([source[:, first, :], source[:, second, :]], axis=-1)
            high, low = split(values.reshape(size, 256))
            result = dot(high_ref[...], high) + (dot(high_ref[...], low) + dot(low_ref[...], high))
            target[:, first, :] = result[:, 0:128].reshape(VARIABLES, 16, 128)
            target[:, second, :] = result[:, 128:256].reshape(VARIABLES, 16, 128)
            return carry

        lax.fori_loop(0, CELLS // 32, chunk, 0)

    project(kl1, kl2, cells, proj)

    def run(fast):
        def component(v, carry):
            pull, push = columns_ref[v, 0], columns_ref[v, 1]

            def fluxes(i, carry):
                rows = pl.ds(pl.multiple_of(8 * i, 8), 8)
                velocity = velocity_ref[rows, :]
                base = proj[v, rows, :]
                source = pressure_ref[rows, :] * (pull + velocity * push)
                plus_ref[rows, :] = (velocity + speed) * base + source
                minus_ref[rows, :] = (velocity - speed) * base + source
                return carry

            lax.fori_loop(0, 35, fluxes, 0, unroll=5)

            def differences(i, carry):
                row = pl.multiple_of(8 * i, 8)
                for source, target in ((plus_ref, dplus_ref), (minus_ref, dminus_ref)):
                    target[pl.ds(row, 8), :] = source[pl.ds(row + 1, 8), :] - source[pl.ds(row, 8), :]
                return carry

            lax.fori_loop(0, 35, differences, 0, unroll=5)

            def faces(i, carry):
                row = pl.multiple_of(8 * i, 8) + 7

                def at(ref, by):
                    return ref[pl.ds(row + by, 8), :]

                gain = correction(
                    at(dplus_ref, -2), at(dplus_ref, -1), at(dplus_ref, 0), at(dplus_ref, 1), fast
                )
                loss = correction(
                    at(dminus_ref, 2), at(dminus_ref, 1), at(dminus_ref, 0), at(dminus_ref, -1), fast
                )
                sums[v, pl.ds(row - 7, 8), :] = at(plus_ref, 0) + at(minus_ref, 1) + (gain - loss)
                return carry

            lax.fori_loop(0, TILES, faces, 0, unroll=3)
            sums[v, 8 * TILES : FACES, :] = jnp.zeros((FACES - 8 * TILES, 128), F32)
            return carry

        lax.fori_loop(0, VARIABLES, component, 0)

    @pl.when(safe)
    def _():
        run(True)

    @pl.when(jnp.logical_not(safe))
    def _():
        run(False)

    project(kr1, kr2, sums, proj)

    def turn_back(v, carry):
        for t in range(2):
            after = proj[v, pl.ds(128 * t + 1, 128), :]
            out_ref[t, v] = (after - proj[v, pl.ds(128 * t, 128), :]).T
        return carry

    lax.fori_loop(0, VARIABLES, turn_back, 0)


def weno(shocked, columns, left, right, pencils, halo):
    size = VARIABLES * GROUP
    return pl.pallas_call(
        weno_body,
        out_shape=jax.ShapeDtypeStruct((2, VARIABLES, PENCILS, 128), F32),
        in_specs=[SMEM, SMEM] + [VMEM] * 5,
        out_specs=VMEM,
        scratch_shapes=[
            pltpu.VMEM((VARIABLES, CELLS, 128), F32),
            pltpu.VMEM((VARIABLES, PENCILS, 128), F32),
            pltpu.VMEM((CELLS, 128), F32),
            pltpu.VMEM((CELLS, 128), F32),
            pltpu.VMEM((VARIABLES, CELLS, 128), F32),
            pltpu.VMEM((CELLS, 128), F32),
            pltpu.VMEM((CELLS, 128), F32),
            pltpu.VMEM((CELLS, 128), F32),
            pltpu.VMEM((CELLS, 128), F32),
            pltpu.VMEM((VARIABLES, FACES, 128), F32),
        ]
        + [pltpu.VMEM((size, size), BF16)] * 4,
        cost_estimate=pl.CostEstimate(
            flops=200_000_000, bytes_accessed=4_000_000, transcendentals=0
        ),
        name="weno",
    )(shocked, columns, shocked.reshape(1, PENCILS), left, right, pencils, halo)


def central_body(
    list_ref, count_ref, u_ref, up_ref, down_ref, zhalo_ref, weno_ref,
    zcoef_ref, hcoef_ref,
    out_ref,
    yhalo, zhalo, hx_ref, replaced, mask_ref, v1_ref, p_ref, stage, along_z, along_y,
):
    x = pl.program_id(0)

    def state(read):
        density = read(0)
        for v in range(1, SPECIES):
            density = density + read(v)
        inverse = 1.0 / density
        m0, m1, m2 = read(9), read(10), read(11)
        pressure = 0.4 * (read(12) - read(13) - 0.5 * (m0 * m0 + m1 * m1 + m2 * m2) * inverse)
        return m1 * inverse, m2 * inverse, pressure

    def flux(value, velocity, pressure, v, normal):
        if v == SPECIES + 3:
            return (value + pressure) * velocity
        if v == SPECIES + normal:
            return value * velocity + pressure
        return value * velocity

    @pl.when(x == 0)
    def _():
        for side, source in enumerate((up_ref, down_ref)):
            for t in range(2):
                velocity, _, pressure = state(lambda v: source[t, v])
                for v in range(VARIABLES):
                    yhalo[side, t, v] = flux(source[t, v], velocity, pressure, v, 1)
        _, velocity, pressure = state(lambda v: zhalo_ref[v])
        for v in range(VARIABLES):
            high, low = split(flux(zhalo_ref[v], velocity, pressure, v, 2))
            zhalo[v, :, 0:128] = high
            zhalo[v, :, 128:256] = low
        hx_ref[...] = jnp.zeros((256, CZ), BF16)
        mask_ref[...] = jnp.zeros((ROWS, 128), F32)
        flat = replaced.reshape(2, VARIABLES * ROWS, 128)
        packed = weno_ref.reshape(2, VARIABLES * PENCILS, 128)

        def scatter(p, carry):
            row = list_ref[p]
            mask_ref[pl.ds(row, 1), :] = jnp.ones((1, 128), F32)
            for t in range(2):
                for v in range(VARIABLES):
                    flat[t, pl.ds(row + v * ROWS, 1), :] = packed[t, pl.ds(p + v * PENCILS, 1), :]
            return carry

        lax.fori_loop(0, count_ref[0], scatter, 0)

    @pl.when(x > 0)
    def _():
        for part in range(2):
            old = pl.ds(pl.multiple_of(128 * part + 16 * x - 16, 16), 16)
            hx_ref[old, :] = jnp.zeros((16, CZ), BF16)

    for part in range(2):
        new = pl.ds(pl.multiple_of(128 * part + 16 * x, 16), 16)
        hx_ref[new, :] = hcoef_ref[...]

    for t in range(2):
        cut = slice(128 * t, 128 * t + 128)
        velocity1, velocity2, pressure = state(lambda v: u_ref[v, 0, :, cut])
        v1_ref[t] = velocity1
        p_ref[t] = pressure
        for v in range(VARIABLES):
            high, low = split(flux(u_ref[v, 0, :, cut], velocity2, pressure, v, 2))
            stage[v, :, cut] = high
            stage[v, :, 256 + 128 * t : 384 + 128 * t] = low

    rows = VARIABLES * CY
    along_z[...] = dot(
        jnp.concatenate(
            [stage[...].reshape(rows, 512), zhalo[...].reshape(rows, 256)], axis=1
        ),
        jnp.concatenate([zcoef_ref[...], zcoef_ref[...], hx_ref[...]], axis=0),
    ).reshape(VARIABLES, CY, CZ)

    hit = mask_ref[pl.ds(pl.multiple_of(CY * x, CY), CY), :] > 0.5
    for v in range(VARIABLES):
        for t in range(2):
            cut = slice(128 * t, 128 * t + 128)
            buffer = along_y.at[v % 2, t]
            value = u_ref[v, 0, :, cut]
            buffer[5:8, :] = yhalo[0, t, v, pl.ds(3 * x, 3), :]
            buffer[8:72, :] = flux(value, v1_ref[t], p_ref[t], v, 1)
            buffer[72:75, :] = yhalo[1, t, v, pl.ds(3 * x, 3), :]

            def at(by):
                return buffer[8 + by : 72 + by, :]

            y_term = 45.0 * (at(1) - at(-1)) - 9.0 * (at(2) - at(-2)) + (at(3) - at(-3))
            z_term = jnp.where(hit, replaced[t, v, x], along_z[v, :, cut])
            out_ref[v, 0, :, cut] = value - SCALE * (y_term + z_term)


def central(shocked, live_count, conserved, up, down, zhalo, terms, coefs):
    return pl.pallas_call(
        central_body,
        grid=(CX,),
        out_shape=jax.ShapeDtypeStruct(conserved.shape, F32),
        in_specs=[
            SMEM,
            SMEM,
            pl.BlockSpec((VARIABLES, 1, CY, CZ), lambda x: (0, x, 0, 0)),
        ]
        + [VMEM] * 6,
        out_specs=pl.BlockSpec((VARIABLES, 1, CY, CZ), lambda x: (0, x, 0, 0)),
        scratch_shapes=[
            pltpu.VMEM((2, 2, VARIABLES, 3 * CX, 128), F32),
            pltpu.VMEM((VARIABLES, CY, 256), BF16),
            pltpu.VMEM((256, CZ), BF16),
            pltpu.VMEM((2, VARIABLES, CX, CY, 128), F32),
            pltpu.VMEM((ROWS, 128), F32),
            pltpu.VMEM((2, CY, 128), F32),
            pltpu.VMEM((2, CY, 128), F32),
            pltpu.VMEM((VARIABLES, CY, 512), BF16),
            pltpu.VMEM((VARIABLES, CY, CZ), F32),
            pltpu.VMEM((2, 2, 80, 128), F32),
        ],
        name="central",
    )(shocked, live_count, conserved, up, down, zhalo, terms, *coefs)


@functools.cache
def coefficients():
    weight = {1: 45.0, -1: -45.0, 2: -9.0, -2: 9.0, 3: 1.0, -3: -1.0}

    def coef(offset):
        return weight.get(offset, 0.0)

    zcoef = np.array([[coef(c - k) for k in range(CZ)] for c in range(CZ)])
    cells = [-3, -2, -1, CZ, CZ + 1, CZ + 2]
    hcoef = np.zeros((16, CZ))
    for j, c in enumerate(cells):
        for k in range(CZ):
            hcoef[j, k] = coef(c - k)
    return zcoef, hcoef


def on_device(conserved, char_left, char_right, shock_list, shock_count):
    shocked = shock_list.reshape(PENCILS)
    live_count = shock_count.reshape(1)
    pencils, up, down, zpack = pack(conserved, shocked)
    zhalo = lax.ppermute(zpack, "gz", [(0, 1), (1, 0)])
    count = lax.axis_size("gy")
    from_below = lax.ppermute(up, "gy", [(i, (i + 1) % count) for i in range(count)])
    from_above = lax.ppermute(down, "gy", [((i + 1) % count, i) for i in range(count)])
    columns = 0.5 * char_left[:, SPECIES + 2 : SPECIES + 4]
    terms = weno(shocked, columns, char_left, char_right, pencils, zhalo)
    coefs = [jnp.asarray(m, BF16) for m in coefficients()]
    return central(
        shocked, live_count, conserved, from_below, from_above, zhalo, terms, coefs
    )


def solution(mesh):
    placed = (P(None, "gx", "gy", "gz"), P(), P(), P("gx", "gy", "gz", None), P("gx", "gy", "gz"))
    return jax.shard_map(
        on_device, mesh=mesh, in_specs=placed, out_specs=P(None, "gx", "gy", "gz"), check_vma=False
    )
```

```python
import functools

import jax
import jax.numpy as jnp
import numpy as np
from jax import lax
from jax.experimental import pallas as pl
from jax.experimental.pallas import tpu as pltpu
from jax.sharding import PartitionSpec as P

SPECIES = 9
VARIABLES = 14
CX, CY, CZ = 8, 64, 256
ROWS = CX * CY
PENCILS = 128
GROUP = 16
SIZE = VARIABLES * GROUP
CELLS = 280
TILES = 33
EPS = 0.75e-6
SCALE = 0.2 / 60.0

F32 = jnp.float32
BF16 = jnp.bfloat16
VMEM = pl.BlockSpec(memory_space=pltpu.VMEM)
SMEM = pl.BlockSpec(memory_space=pltpu.SMEM)
ANY = pl.BlockSpec(memory_space=pl.ANY)


def lanes(shape):
    return lax.broadcasted_iota(jnp.int32, shape, len(shape) - 1)


def split(values):
    high = values.astype(BF16)
    low = (values - high.astype(F32)).astype(BF16)
    return high, low


def dot(left, right):
    return jnp.dot(left, right, preferred_element_type=F32)


def state_of(read):
    density = read(0)
    for v in range(1, SPECIES):
        density = density + read(v)
    inverse = 1.0 / density
    m0, m1, m2 = read(9), read(10), read(11)
    squares = m0 * m0 + m1 * m1 + m2 * m2
    pressure = 0.4 * (read(12) - read(13) - 0.5 * squares * inverse)
    return m1 * inverse, m2 * inverse, pressure


def flux(value, velocity, pressure, v, normal):
    if v == SPECIES + 3:
        return (value + pressure) * velocity
    if v == SPECIES + normal:
        return value * velocity + pressure
    return value * velocity


def expand(matrix, scale, target):
    row = lax.broadcasted_iota(jnp.int32, (SIZE, SIZE), 0)
    column = lax.broadcasted_iota(jnp.int32, (SIZE, SIZE), 1)
    same = (row & (GROUP - 1)) == (column & (GROUP - 1))
    spread = (
        lax.broadcasted_iota(jnp.int32, (SIZE, VARIABLES), 0) // GROUP
        == lax.broadcasted_iota(jnp.int32, (SIZE, VARIABLES), 1)
    ).astype(BF16)
    gather = (
        lax.broadcasted_iota(jnp.int32, (VARIABLES, SIZE), 1) // GROUP
        == lax.broadcasted_iota(jnp.int32, (VARIABLES, SIZE), 0)
    ).astype(BF16)
    for part, places in zip(split(scale * matrix), ((0, 1), (2,))):
        wide = dot(spread, dot(part, gather).astype(BF16))
        wide = jnp.where(same, wide, 0.0).astype(BF16)
        for place in places:
            target[:, SIZE * place : SIZE * place + SIZE] = wide


def project(matrix, values):
    high, low = split(values)
    return dot(matrix[...], jnp.concatenate([high, low, high], axis=0))


def prepare_body(
    list_ref, where_ref, left_ref, right_ref, u_hbm,
    proj, velocity_ref, pressure_ref, speed_ref, yflux, zflux, kr_out,
    u_ref, rows_ref, cells, kl_ref, up_send, down_send, z_send, y_recv, z_recv,
    load_sems, send_sems, recv_sems,
):
    loads = []

    def load(index, t, x, y):
        copy = pltpu.make_async_copy(
            u_hbm.at[:, x, y, pl.ds(128 * t, 128)], u_ref.at[t, :, x, y], load_sems.at[index]
        )
        copy.start()
        loads.append(copy)

    every = pl.ds(0, CX)
    for t in range(2):
        load(len(loads), t, every, pl.ds(0, 8))
        load(len(loads), t, every, pl.ds(CY - 8, 8))
    for x in range(CX):
        for t in range(2):
            load(len(loads), t, pl.ds(x, 1), pl.ds(8, CY - 16))

    gy, gz = lax.axis_index("gy"), lax.axis_index("gz")
    ny = lax.axis_size("gy")
    above, below = {"gy": lax.rem(gy + 1, ny)}, {"gy": lax.rem(gy + ny - 1, ny)}
    beside = {"gz": 1 - gz}
    barrier = pltpu.get_barrier_semaphore()
    for device in (above, below, beside):
        pl.semaphore_signal(barrier, inc=1, device_id=device, device_id_type=pl.DeviceIdType.MESH)

    def remote(index, source, target, device):
        return pltpu.make_async_remote_copy(
            src_ref=source,
            dst_ref=target,
            send_sem=send_sems.at[index],
            recv_sem=recv_sems.at[index],
            device_id=device,
            device_id_type=pl.DeviceIdType.MESH,
        )

    for copy in loads[:4]:
        copy.wait()

    def y_ends(v, carry):
        for t in range(2):
            for x in range(CX):
                down_send[t, v, 3 * x : 3 * x + 3, :] = u_ref[t, v, x, 0:3, :]
                up_send[t, v, 3 * x : 3 * x + 3, :] = u_ref[t, v, x, CY - 3 : CY, :]
        return carry

    lax.fori_loop(0, VARIABLES, y_ends, 0)
    expand(left_ref[...], 0.5, kl_ref)
    expand(right_ref[...], 60.0, kr_out)
    pl.semaphore_wait(barrier, 3)
    up = remote(0, up_send, y_recv.at[0], above)
    down = remote(1, down_send, y_recv.at[1], below)
    up.start()
    down.start()

    lane = lanes((CY, 128))
    for x in range(CX):
        loads[4 + 2 * x].wait()
        loads[5 + 2 * x].wait()

        def z_ends(v, carry, x=x):
            ends = jnp.where(lane < 64, u_ref[0, v, x], u_ref[1, v, x])
            ends = pltpu.roll(ends, 16 * x + 3, 1)
            if x == 0:
                z_send[v] = ends
            else:
                z_send[v] = jnp.where(lane < 16 * x, z_send[v], ends)
            return carry

        lax.fori_loop(0, VARIABLES, z_ends, 0, unroll=2)

    flat = u_ref.reshape(2, VARIABLES * ROWS, 128)
    packed = rows_ref.reshape(2, VARIABLES * PENCILS, 128)

    def gather(p, carry):
        row = list_ref[p]
        for t in range(2):
            for v in range(VARIABLES):
                packed[t, pl.ds(p + v * PENCILS, 1), :] = flat[t, pl.ds(row + v * ROWS, 1), :]
        return carry

    lax.fori_loop(0, 8, gather, 0, unroll=2)
    ends = remote(2, z_send, z_recv, beside)
    ends.start()
    lax.fori_loop(8, PENCILS, gather, 0, unroll=2)

    def turn(v, carry):
        for t in range(2):
            cells[v, 8 + 128 * t : 136 + 128 * t, :] = rows_ref[t, v].T
        return carry

    lax.fori_loop(0, VARIABLES, turn, 0)

    def wave(i, peak):
        rows = pl.ds(pl.multiple_of(8 * i, 8), 8)
        _, velocity, pressure = state_of(lambda v: cells[v, rows, :])
        velocity_ref[rows, :] = velocity
        pressure_ref[rows, :] = pressure
        return jnp.maximum(peak, jnp.abs(velocity))

    peak = lax.fori_loop(1, 33, wave, jnp.zeros((8, 128), F32), unroll=2)

    def chunk(i, carry):
        first = pl.ds(pl.multiple_of(32 * i + 8, 8), 16)
        second = pl.ds(pl.multiple_of(32 * i + 24, 8), 16)
        values = jnp.concatenate([cells[:, first, :], cells[:, second, :]], axis=-1)
        result = project(kl_ref, values.reshape(SIZE, 256))
        proj[:, first, :] = result[:, 0:128].reshape(VARIABLES, 16, 128)
        proj[:, second, :] = result[:, 128:256].reshape(VARIABLES, 16, 128)
        return carry

    lax.fori_loop(0, CZ // 32, chunk, 0)

    ends.wait()
    halo_rows = z_recv.reshape(VARIABLES * CY, 128)
    fetched = rows_ref.at[0].reshape(VARIABLES * PENCILS, 128)

    def fetch(p, carry):
        y = list_ref[p] % CY
        for v in range(VARIABLES):
            fetched[pl.ds(p + v * PENCILS, 1), :] = halo_rows[pl.ds(y + v * CY, 1), :]
        return carry

    lax.fori_loop(0, PENCILS, fetch, 0, unroll=2)
    own_x = jnp.broadcast_to(where_ref[...] // CY, (16, 128))

    def turn_ends(v, carry):
        turned = rows_ref[0, v].T
        near = turned[0:16]
        for x in range(1, CX):
            near = jnp.where(own_x == x, turned[16 * x : 16 * x + 16], near)
        cells[v, 0:5, :] = near[0:5]
        cells[v, 5:8, :] = near[0:3]
        cells[v, 264:267, :] = near[3:6]
        cells[v, 267:272, :] = near[0:5]
        return carry

    lax.fori_loop(0, VARIABLES, turn_ends, 0, unroll=2)
    peak = wave(0, peak)
    peak = wave(33, peak)
    speed_ref[...] = jnp.broadcast_to(jnp.max(peak, axis=0, keepdims=True) + 1.0, (8, 128))
    values = jnp.concatenate([cells[:, 0:8, :], cells[:, 264:272, :]], axis=1)
    result = project(kl_ref, values.reshape(SIZE, 128)).reshape(VARIABLES, 16, 128)
    proj[:, 0:8, :] = result[:, 0:8]
    proj[:, 264:272, :] = result[:, 8:16]

    _, velocity, pressure = state_of(lambda v: z_recv[v])
    for v in range(VARIABLES):
        high, low = split(flux(z_recv[v], velocity, pressure, v, 2))
        zflux[v, :, 0:128] = high
        zflux[v, :, 128:256] = low

    up.wait()
    down.wait()
    for side in range(2):
        for t in range(2):
            velocity, _, pressure = state_of(lambda v: y_recv[side, t, v])
            for v in range(VARIABLES):
                yflux[side, t, v] = flux(y_recv[side, t, v], velocity, pressure, v, 1)


def prepare(shocked, left, right, conserved):
    return pl.pallas_call(
        prepare_body,
        out_shape=(
            jax.ShapeDtypeStruct((VARIABLES, CELLS, 128), F32),
            jax.ShapeDtypeStruct((CELLS, 128), F32),
            jax.ShapeDtypeStruct((CELLS, 128), F32),
            jax.ShapeDtypeStruct((8, 128), F32),
            jax.ShapeDtypeStruct((2, 2, VARIABLES, 3 * CX, 128), F32),
            jax.ShapeDtypeStruct((VARIABLES, CY, 256), BF16),
            jax.ShapeDtypeStruct((SIZE, 3 * SIZE), BF16),
        ),
        in_specs=[SMEM, VMEM, VMEM, VMEM, ANY],
        out_specs=(VMEM,) * 7,
        scratch_shapes=[
            pltpu.VMEM((2, VARIABLES, CX, CY, 128), F32),
            pltpu.VMEM((2, VARIABLES, PENCILS, 128), F32),
            pltpu.VMEM((VARIABLES, 272, 128), F32),
            pltpu.VMEM((SIZE, 3 * SIZE), BF16),
            pltpu.VMEM((2, VARIABLES, 3 * CX, 128), F32),
            pltpu.VMEM((2, VARIABLES, 3 * CX, 128), F32),
            pltpu.VMEM((VARIABLES, CY, 128), F32),
            pltpu.VMEM((2, 2, VARIABLES, 3 * CX, 128), F32),
            pltpu.VMEM((VARIABLES, CY, 128), F32),
            pltpu.SemaphoreType.DMA((4 + 2 * CX,)),
            pltpu.SemaphoreType.DMA((3,)),
            pltpu.SemaphoreType.DMA((3,)),
        ],
        compiler_params=pltpu.CompilerParams(collective_id=0, has_side_effects=True),
        name="prepare",
    )(shocked, shocked.reshape(1, PENCILS), left, right, conserved)


def weno_terms(columns_ref, proj, velocity_ref, pressure_ref, speed_ref, kr_ref, scratch):
    plus_ref, minus_ref, terms, sums, across, terms_out = scratch
    speed = speed_ref[...]

    def component(v, carry):
        pull, push = columns_ref[v, 0], columns_ref[v, 1]

        def fluxes(i, carry):
            rows = pl.ds(pl.multiple_of(8 * i, 8), 8)
            velocity = velocity_ref[rows, :]
            base = proj[v, rows, :]
            source = pressure_ref[rows, :] * (pull + velocity * push)
            plus_ref[rows, :] = (velocity + speed) * base + source
            minus_ref[rows, :] = (velocity - speed) * base + source
            return carry

        lax.fori_loop(0, 34, fluxes, 0, unroll=2)

        def pairs(i, carry):
            row = pl.multiple_of(8 * i, 8)
            for side, source in enumerate((plus_ref, minus_ref)):
                middle = source[pl.ds(row + 6, 8), :]
                x = middle - source[pl.ds(row + 5, 8), :]
                y = source[pl.ds(row + 7, 8), :] - middle
                xx, xy, yy = x * x, x * y, y * y
                ex, ey = xx + EPS, yy + EPS
                cross = 2.75 * xy
                lean = 1.0 / ((ex + 2.5 * yy) - cross)
                even = 1.0 / ((ex + yy) - 1.25 * xy)
                back = 1.0 / ((2.5 * xx + ey) - cross)
                x2, y2 = x + x, y + y
                if side == 0:
                    w0, w1, w2 = lean * lean, 6.0 * (even * even), 3.0 * (back * back)
                    n0, n1, n2 = 5.0 * y - x2, x + y2, (x2 + x2) - y
                else:
                    w0, w1, w2 = back * back, 6.0 * (even * even), 3.0 * (lean * lean)
                    n0, n1, n2 = 5.0 * x - y2, y + x2, (y2 + y2) - x
                for k, value in enumerate((w0, w1, w2, w0 * n0, w1 * n1, w2 * n2)):
                    terms[6 * side + k, pl.ds(row, 8), :] = value
            return carry

        lax.fori_loop(0, TILES, pairs, 0, unroll=3)

        def faces(i, carry):
            row = pl.multiple_of(8 * i, 8)

            def at(k, by):
                return terms[k, pl.ds(row + by, 8), :]

            gain = (at(3, 0) + at(4, 1) + at(5, 2)) / (at(0, 0) + at(1, 1) + at(2, 2))
            loss = (at(9, 3) + at(10, 2) + at(11, 1)) / (at(6, 3) + at(7, 2) + at(8, 1))
            base = plus_ref[pl.ds(row + 7, 8), :] + minus_ref[pl.ds(row + 8, 8), :]
            sums[v, pl.ds(row, 8), :] = base + (gain - loss) * (1.0 / 6.0)
            return carry

        lax.fori_loop(0, TILES, faces, 0, unroll=3)
        return carry

    lax.fori_loop(0, VARIABLES, component, 0)

    def chunk(i, carry):
        start = pl.multiple_of(32 * i, 8)

        def change(by):
            return sums[:, pl.ds(start + by + 1, 16), :] - sums[:, pl.ds(start + by, 16), :]

        values = jnp.concatenate([change(0), change(16)], axis=-1)
        result = project(kr_ref, values.reshape(SIZE, 256))
        for k in range(2):
            rows = pl.ds(pl.multiple_of(start + 16 * k, 8), 16)
            across[:, rows, :] = result[:, 128 * k : 128 * k + 128].reshape(VARIABLES, 16, 128)
        return carry

    lax.fori_loop(0, CZ // 32, chunk, 0)

    def turn_back(v, carry):
        for t in range(2):
            terms_out[t, v] = across[v, 128 * t : 128 * t + 128, :].T
        return carry

    lax.fori_loop(0, VARIABLES, turn_back, 0)


def advance_body(
    list_ref, count_ref, columns_ref, u_ref,
    proj, velocity_ref, pressure_ref, speed_ref, yflux, zflux, kr_ref, zcoef_ref, hcoef_ref,
    out_ref,
    hx_ref, replaced, mask_ref, v1_ref, p_ref, stage, along_z, along_y, *scratch,
):
    x = pl.program_id(0)

    @pl.when(x == 0)
    def _():
        weno_terms(columns_ref, proj, velocity_ref, pressure_ref, speed_ref, kr_ref, scratch)
        hx_ref[...] = jnp.zeros((256, CZ), BF16)
        mask_ref[...] = jnp.zeros((ROWS, 128), F32)
        flat = replaced.reshape(2, VARIABLES * ROWS, 128)
        packed = scratch[-1].reshape(2, VARIABLES * PENCILS, 128)

        def scatter(p, carry):
            row = list_ref[p]
            mask_ref[pl.ds(row, 1), :] = jnp.ones((1, 128), F32)
            for t in range(2):
                for v in range(VARIABLES):
                    flat[t, pl.ds(row + v * ROWS, 1), :] = packed[t, pl.ds(p + v * PENCILS, 1), :]
            return carry

        lax.fori_loop(0, count_ref[0], scatter, 0)

    @pl.when(x > 0)
    def _():
        for part in range(2):
            old = pl.ds(pl.multiple_of(128 * part + 16 * x - 16, 16), 16)
            hx_ref[old, :] = jnp.zeros((16, CZ), BF16)

    for part in range(2):
        new = pl.ds(pl.multiple_of(128 * part + 16 * x, 16), 16)
        hx_ref[new, :] = hcoef_ref[...]

    for t in range(2):
        cut = slice(128 * t, 128 * t + 128)
        velocity1, velocity2, pressure = state_of(lambda v: u_ref[v, 0, :, cut])
        v1_ref[t] = velocity1
        p_ref[t] = pressure
        for v in range(VARIABLES):
            high, low = split(flux(u_ref[v, 0, :, cut], velocity2, pressure, v, 2))
            stage[v, :, cut] = high
            stage[v, :, 256 + 128 * t : 384 + 128 * t] = low

    rows = VARIABLES * CY
    along_z[...] = dot(
        jnp.concatenate([stage[...].reshape(rows, 512), zflux[...].reshape(rows, 256)], axis=1),
        jnp.concatenate([zcoef_ref[...], zcoef_ref[...], hx_ref[...]], axis=0),
    ).reshape(VARIABLES, CY, CZ)

    hit = mask_ref[pl.ds(pl.multiple_of(CY * x, CY), CY), :] > 0.5
    for v in range(VARIABLES):
        for t in range(2):
            cut = slice(128 * t, 128 * t + 128)
            buffer = along_y.at[v % 2, t]
            value = u_ref[v, 0, :, cut]
            buffer[5:8, :] = yflux[0, t, v, pl.ds(3 * x, 3), :]
            buffer[8:72, :] = flux(value, v1_ref[t], p_ref[t], v, 1)
            buffer[72:75, :] = yflux[1, t, v, pl.ds(3 * x, 3), :]

            def at(by):
                return buffer[8 + by : 72 + by, :]

            y_term = 45.0 * (at(1) - at(-1)) - 9.0 * (at(2) - at(-2)) + (at(3) - at(-3))
            z_term = jnp.where(hit, replaced[t, v, x], along_z[v, :, cut])
            out_ref[v, 0, :, cut] = value - SCALE * (y_term + z_term)


def advance(shocked, live_count, columns, conserved, prepared, coefs):
    block = pl.BlockSpec((VARIABLES, 1, CY, CZ), lambda x: (0, x, 0, 0))
    return pl.pallas_call(
        advance_body,
        grid=(CX,),
        out_shape=jax.ShapeDtypeStruct(conserved.shape, F32),
        in_specs=[SMEM, SMEM, SMEM, block] + [VMEM] * 9,
        out_specs=block,
        scratch_shapes=[
            pltpu.VMEM((256, CZ), BF16),
            pltpu.VMEM((2, VARIABLES, CX, CY, 128), F32),
            pltpu.VMEM((ROWS, 128), F32),
            pltpu.VMEM((2, CY, 128), F32),
            pltpu.VMEM((2, CY, 128), F32),
            pltpu.VMEM((VARIABLES, CY, 512), BF16),
            pltpu.VMEM((VARIABLES, CY, CZ), F32),
            pltpu.VMEM((2, 2, 80, 128), F32),
            pltpu.VMEM((CELLS, 128), F32),
            pltpu.VMEM((CELLS, 128), F32),
            pltpu.VMEM((12, CELLS, 128), F32),
            pltpu.VMEM((VARIABLES, CELLS, 128), F32),
            pltpu.VMEM((VARIABLES, CZ, 128), F32),
            pltpu.VMEM((2, VARIABLES, PENCILS, 128), F32),
        ],
        name="advance",
    )(shocked, live_count, columns, conserved, *prepared, *coefs)


@functools.cache
def coefficients():
    weight = {1: 45.0, -1: -45.0, 2: -9.0, -2: 9.0, 3: 1.0, -3: -1.0}

    def coef(offset):
        return weight.get(offset, 0.0)

    zcoef = np.array([[coef(c - k) for k in range(CZ)] for c in range(CZ)])
    cells = [-3, -2, -1, CZ, CZ + 1, CZ + 2]
    hcoef = np.zeros((16, CZ))
    for j, c in enumerate(cells):
        for k in range(CZ):
            hcoef[j, k] = coef(c - k)
    return zcoef, hcoef


def on_device(conserved, char_left, char_right, shock_list, shock_count):
    shocked = shock_list.reshape(PENCILS)
    live_count = shock_count.reshape(1)
    prepared = prepare(shocked, char_left, char_right, conserved)
    columns = 0.5 * char_left[:, SPECIES + 2 : SPECIES + 4]
    coefs = [jnp.asarray(m, BF16) for m in coefficients()]
    return advance(shocked, live_count, columns, conserved, prepared, coefs)


def solution(mesh):
    placed = (P(None, "gx", "gy", "gz"), P(), P(), P("gx", "gy", "gz", None), P("gx", "gy", "gz"))
    return jax.shard_map(
        on_device, mesh=mesh, in_specs=placed, out_specs=P(None, "gx", "gy", "gz"), check_vma=False
    )
```

```python
import functools

import jax
import jax.numpy as jnp
import numpy as np
from jax import lax
from jax.experimental import pallas as pl
from jax.experimental.pallas import tpu as pltpu
from jax.sharding import PartitionSpec as P

SPECIES = 9
VARIABLES = 14
CX, CY, CZ = 8, 64, 256
ROWS = CX * CY
PENCILS = 128
GROUP = 16
SIZE = VARIABLES * GROUP
CELLS = 280
TILES = 33
EPS = 0.75e-6
SCALE = 0.2 / 60.0

F32 = jnp.float32
BF16 = jnp.bfloat16
VMEM = pl.BlockSpec(memory_space=pltpu.VMEM)
SMEM = pl.BlockSpec(memory_space=pltpu.SMEM)
HBM = pl.BlockSpec(memory_space=pltpu.HBM)


def lanes(shape):
    return lax.broadcasted_iota(jnp.int32, shape, len(shape) - 1)


def split(values):
    high = values.astype(BF16)
    low = (values - high.astype(F32)).astype(BF16)
    return high, low


def dot(left, right):
    return jnp.dot(left, right, preferred_element_type=F32)


def state_of(read):
    density = read(0)
    for v in range(1, SPECIES):
        density = density + read(v)
    inverse = 1.0 / density
    m0, m1, m2 = read(9), read(10), read(11)
    squares = m0 * m0 + m1 * m1 + m2 * m2
    pressure = 0.4 * (read(12) - read(13) - 0.5 * squares * inverse)
    return m1 * inverse, m2 * inverse, pressure


def flux(value, velocity, pressure, v, normal):
    if v == SPECIES + 3:
        return (value + pressure) * velocity
    if v == SPECIES + normal:
        return value * velocity + pressure
    return value * velocity


def expand(matrix, scale, target):
    row = lax.broadcasted_iota(jnp.int32, (SIZE, SIZE), 0)
    column = lax.broadcasted_iota(jnp.int32, (SIZE, SIZE), 1)
    same = (row & (GROUP - 1)) == (column & (GROUP - 1))
    spread = (
        lax.broadcasted_iota(jnp.int32, (SIZE, VARIABLES), 0) // GROUP
        == lax.broadcasted_iota(jnp.int32, (SIZE, VARIABLES), 1)
    ).astype(BF16)
    gather = (
        lax.broadcasted_iota(jnp.int32, (VARIABLES, SIZE), 1) // GROUP
        == lax.broadcasted_iota(jnp.int32, (VARIABLES, SIZE), 0)
    ).astype(BF16)
    for part, places in zip(split(scale * matrix), ((0, 1), (2,))):
        wide = dot(spread, dot(part, gather).astype(BF16))
        wide = jnp.where(same, wide, 0.0).astype(BF16)
        for place in places:
            target[:, SIZE * place : SIZE * place + SIZE] = wide


def project(matrix, values):
    high, low = split(values)
    return dot(matrix[...], jnp.concatenate([high, low, high], axis=0))


def prepare_body(
    list_ref, where_ref, left_ref, right_ref, u_hbm,
    u_ref, proj, velocity_ref, pressure_ref, speed_ref, yflux, zflux, kr_out, pull_ref,
    rows_ref, cells, kl_ref, up_send, down_send, z_send, y_recv, z_recv,
    load_sems, send_sems, recv_sems,
):
    loads = []

    def load(index, t, x, y):
        copy = pltpu.make_async_copy(
            u_hbm.at[:, x, y, pl.ds(128 * t, 128)], u_ref.at[t, :, x, y], load_sems.at[index]
        )
        copy.start()
        loads.append(copy)

    every = pl.ds(0, CX)
    for t in range(2):
        load(len(loads), t, every, pl.ds(0, 8))
        load(len(loads), t, every, pl.ds(CY - 8, 8))
    for x in range(CX):
        for t in range(2):
            load(len(loads), t, pl.ds(x, 1), pl.ds(8, CY - 16))

    gy, gz = lax.axis_index("gy"), lax.axis_index("gz")
    ny = lax.axis_size("gy")
    above, below = {"gy": lax.rem(gy + 1, ny)}, {"gy": lax.rem(gy + ny - 1, ny)}
    beside = {"gz": 1 - gz}
    barrier = pltpu.get_barrier_semaphore()
    for device in (above, below, beside):
        pl.semaphore_signal(barrier, inc=1, device_id=device, device_id_type=pl.DeviceIdType.MESH)

    def remote(index, source, target, device):
        return pltpu.make_async_remote_copy(
            src_ref=source,
            dst_ref=target,
            send_sem=send_sems.at[index],
            recv_sem=recv_sems.at[index],
            device_id=device,
            device_id_type=pl.DeviceIdType.MESH,
        )

    for copy in loads[:4]:
        copy.wait()

    def y_ends(v, carry):
        for t in range(2):
            for x in range(CX):
                down_send[t, v, 3 * x : 3 * x + 3, :] = u_ref[t, v, x, 0:3, :]
                up_send[t, v, 3 * x : 3 * x + 3, :] = u_ref[t, v, x, CY - 3 : CY, :]
        return carry

    lax.fori_loop(0, VARIABLES, y_ends, 0)
    expand(left_ref[...], 0.5, kl_ref)
    expand(right_ref[...], 60.0, kr_out)
    for k in range(2):
        at = SPECIES + 2 + k
        pull_ref[k, 0:VARIABLES, :] = jnp.broadcast_to(
            0.5 * left_ref[:, at : at + 1], (VARIABLES, 128)
        )
    pl.semaphore_wait(barrier, 3)
    up = remote(0, up_send, y_recv.at[0], above)
    down = remote(1, down_send, y_recv.at[1], below)
    up.start()
    down.start()

    lane = lanes((CY, 128))
    source = lax.broadcasted_iota(jnp.int32, (CX * 128, 128), 0)
    place = lax.broadcasted_iota(jnp.int32, (CX * 128, 128), 1)
    within = ((source & 127) + 3) & 127
    wanted = jnp.minimum(place & 15, 5)
    select = ((place // 16 == source // 128) & (within == wanted)).astype(BF16)
    select = jnp.concatenate([select, select], axis=0)
    for copy in loads[4:]:
        copy.wait()

    def z_ends(v, carry):
        highs, lows = [], []
        for x in range(CX):
            high, low = split(jnp.where(lane < 64, u_ref[0, v, x], u_ref[1, v, x]))
            highs.append(high)
            lows.append(low)
        z_send[v] = dot(jnp.concatenate(highs + lows, axis=1), select)
        return carry

    lax.fori_loop(0, VARIABLES, z_ends, 0, unroll=7)

    flat = u_ref.reshape(2, VARIABLES * ROWS, 128)
    packed = rows_ref.reshape(2, VARIABLES * PENCILS, 128)

    def gather(p, carry):
        row = list_ref[p]
        for t in range(2):
            for v in range(VARIABLES):
                packed[t, pl.ds(p + v * PENCILS, 1), :] = flat[t, pl.ds(row + v * ROWS, 1), :]
        return carry

    lax.fori_loop(0, 8, gather, 0, unroll=2)
    ends = remote(2, z_send, z_recv, beside)
    ends.start()
    lax.fori_loop(8, PENCILS, gather, 0, unroll=2)

    def turn(v, carry):
        for t in range(2):
            cells[v, 8 + 128 * t : 136 + 128 * t, :] = rows_ref[t, v].T
        return carry

    lax.fori_loop(0, VARIABLES, turn, 0, unroll=2)

    def wave(i, peak):
        rows = pl.ds(pl.multiple_of(8 * i, 8), 8)
        _, velocity, pressure = state_of(lambda v: cells[v, rows, :])
        velocity_ref[rows, :] = velocity
        pressure_ref[rows, :] = pressure
        return jnp.maximum(peak, jnp.abs(velocity))

    peak = lax.fori_loop(1, 33, wave, jnp.zeros((8, 128), F32), unroll=2)

    def chunk(i, carry):
        first = pl.ds(pl.multiple_of(32 * i + 8, 8), 16)
        second = pl.ds(pl.multiple_of(32 * i + 24, 8), 16)
        values = jnp.concatenate([cells[:, first, :], cells[:, second, :]], axis=-1)
        result = project(kl_ref, values.reshape(SIZE, 256))
        proj[:, first, :] = result[:, 0:128].reshape(VARIABLES, 16, 128)
        proj[:, second, :] = result[:, 128:256].reshape(VARIABLES, 16, 128)
        return carry

    lax.fori_loop(0, CZ // 32, chunk, 0, unroll=4)

    ends.wait()
    halo_rows = z_recv.reshape(VARIABLES * CY, 128)
    fetched = rows_ref.at[0].reshape(VARIABLES * PENCILS, 128)

    def fetch(p, carry):
        y = list_ref[p] % CY
        for v in range(VARIABLES):
            fetched[pl.ds(p + v * PENCILS, 1), :] = halo_rows[pl.ds(y + v * CY, 1), :]
        return carry

    lax.fori_loop(0, PENCILS, fetch, 0, unroll=2)
    own_x = jnp.broadcast_to(where_ref[...] // CY, (16, 128))

    def turn_ends(v, carry):
        turned = rows_ref[0, v].T
        near = turned[0:16]
        for x in range(1, CX):
            near = jnp.where(own_x == x, turned[16 * x : 16 * x + 16], near)
        cells[v, 0:5, :] = near[0:5]
        cells[v, 5:8, :] = near[0:3]
        cells[v, 264:267, :] = near[3:6]
        cells[v, 267:272, :] = near[0:5]
        return carry

    lax.fori_loop(0, VARIABLES, turn_ends, 0, unroll=2)
    peak = wave(0, peak)
    peak = wave(33, peak)
    speed_ref[...] = jnp.broadcast_to(jnp.max(peak, axis=0, keepdims=True) + 1.0, (8, 128))
    values = jnp.concatenate([cells[:, 0:8, :], cells[:, 264:272, :]], axis=1)
    result = project(kl_ref, values.reshape(SIZE, 128)).reshape(VARIABLES, 16, 128)
    proj[:, 0:8, :] = result[:, 0:8]
    proj[:, 264:272, :] = result[:, 8:16]

    _, velocity, pressure = state_of(lambda v: z_recv[v])
    for v in range(VARIABLES):
        high, low = split(flux(z_recv[v], velocity, pressure, v, 2))
        zflux[v, :, 0:128] = high
        zflux[v, :, 128:256] = low

    up.wait()
    down.wait()
    for side in range(2):
        for t in range(2):
            velocity, _, pressure = state_of(lambda v: y_recv[side, t, v])
            for v in range(VARIABLES):
                yflux[side, t, v] = flux(y_recv[side, t, v], velocity, pressure, v, 1)


def prepare(shocked, left, right, conserved):
    return pl.pallas_call(
        prepare_body,
        out_shape=(
            pltpu.VMEM((2, VARIABLES, CX, CY, 128), F32),
            pltpu.VMEM((VARIABLES, CELLS, 128), F32),
            pltpu.VMEM((CELLS, 128), F32),
            pltpu.VMEM((CELLS, 128), F32),
            pltpu.VMEM((8, 128), F32),
            pltpu.VMEM((2, 2, VARIABLES, 3 * CX, 128), F32),
            pltpu.VMEM((VARIABLES, CY, 256), BF16),
            pltpu.VMEM((SIZE, 3 * SIZE), BF16),
            pltpu.VMEM((2, 16, 128), F32),
        ),
        in_specs=[SMEM, VMEM, VMEM, VMEM, HBM],
        out_specs=(VMEM,) * 9,
        scratch_shapes=[
            pltpu.VMEM((2, VARIABLES, PENCILS, 128), F32),
            pltpu.VMEM((VARIABLES, 272, 128), F32),
            pltpu.VMEM((SIZE, 3 * SIZE), BF16),
            pltpu.VMEM((2, VARIABLES, 3 * CX, 128), F32),
            pltpu.VMEM((2, VARIABLES, 3 * CX, 128), F32),
            pltpu.VMEM((VARIABLES, CY, 128), F32),
            pltpu.VMEM((2, 2, VARIABLES, 3 * CX, 128), F32),
            pltpu.VMEM((VARIABLES, CY, 128), F32),
            pltpu.SemaphoreType.DMA((4 + 2 * CX,)),
            pltpu.SemaphoreType.DMA((3,)),
            pltpu.SemaphoreType.DMA((3,)),
        ],
        compiler_params=pltpu.CompilerParams(
            collective_id=0, has_side_effects=True, vmem_limit_bytes=46 << 20
        ),
        name="prepare",
    )(shocked, shocked.reshape(1, PENCILS), left, right, conserved)


def weno_terms(pull_ref, proj, velocity_ref, pressure_ref, speed_ref, kr_ref, scratch):
    plus_ref, minus_ref, terms, sums, across, terms_out = scratch
    speed = speed_ref[...]

    def component(v, carry):
        pull = jnp.broadcast_to(pull_ref[0, pl.ds(v, 1), :], (8, 128))
        push = jnp.broadcast_to(pull_ref[1, pl.ds(v, 1), :], (8, 128))

        def fluxes(i, carry):
            rows = pl.ds(pl.multiple_of(8 * i, 8), 8)
            velocity = velocity_ref[rows, :]
            base = proj[v, rows, :]
            source = pressure_ref[rows, :] * (pull + velocity * push)
            plus_ref[rows, :] = (velocity + speed) * base + source
            minus_ref[rows, :] = (velocity - speed) * base + source
            return carry

        lax.fori_loop(0, 34, fluxes, 0, unroll=2)

        def pairs(i, carry):
            row = pl.multiple_of(8 * i, 8)
            for side, source in enumerate((plus_ref, minus_ref)):
                middle = source[pl.ds(row + 6, 8), :]
                x = middle - source[pl.ds(row + 5, 8), :]
                y = source[pl.ds(row + 7, 8), :] - middle
                xx, xy, yy = x * x, x * y, y * y
                ex, ey = xx + EPS, yy + EPS
                cross = 2.75 * xy
                lean = 1.0 / ((ex + 2.5 * yy) - cross)
                even = 1.0 / ((ex + yy) - 1.25 * xy)
                back = 1.0 / ((2.5 * xx + ey) - cross)
                x2, y2 = x + x, y + y
                if side == 0:
                    w0, w1, w2 = lean * lean, 6.0 * (even * even), 3.0 * (back * back)
                    n0, n1, n2 = 5.0 * y - x2, x + y2, (x2 + x2) - y
                else:
                    w0, w1, w2 = back * back, 6.0 * (even * even), 3.0 * (lean * lean)
                    n0, n1, n2 = 5.0 * x - y2, y + x2, (y2 + y2) - x
                for k, value in enumerate((w0, w1, w2, w0 * n0, w1 * n1, w2 * n2)):
                    terms[6 * side + k, pl.ds(row, 8), :] = value
            return carry

        lax.fori_loop(0, TILES, pairs, 0, unroll=33)

        def faces(i, carry):
            row = pl.multiple_of(8 * i, 8)

            def at(k, by):
                return terms[k, pl.ds(row + by, 8), :]

            gain = (at(3, 0) + at(4, 1) + at(5, 2)) / (at(0, 0) + at(1, 1) + at(2, 2))
            loss = (at(9, 3) + at(10, 2) + at(11, 1)) / (at(6, 3) + at(7, 2) + at(8, 1))
            base = plus_ref[pl.ds(row + 7, 8), :] + minus_ref[pl.ds(row + 8, 8), :]
            sums[v, pl.ds(row, 8), :] = base + (gain - loss) * (1.0 / 6.0)
            return carry

        lax.fori_loop(0, TILES, faces, 0, unroll=33)
        return carry

    lax.fori_loop(0, VARIABLES, component, 0)

    def chunk(i, carry):
        start = pl.multiple_of(32 * i, 8)

        def change(by):
            return sums[:, pl.ds(start + by + 1, 16), :] - sums[:, pl.ds(start + by, 16), :]

        values = jnp.concatenate([change(0), change(16)], axis=-1)
        result = project(kr_ref, values.reshape(SIZE, 256))
        for k in range(2):
            rows = pl.ds(pl.multiple_of(start + 16 * k, 8), 16)
            across[:, rows, :] = result[:, 128 * k : 128 * k + 128].reshape(VARIABLES, 16, 128)
        return carry

    lax.fori_loop(0, CZ // 32, chunk, 0, unroll=4)

    def turn_back(v, carry):
        for t in range(2):
            terms_out[t, v] = across[v, 128 * t : 128 * t + 128, :].T
        return carry

    lax.fori_loop(0, VARIABLES, turn_back, 0, unroll=2)


def advance_body(
    list_ref, count_ref, u_ref,
    proj, velocity_ref, pressure_ref, speed_ref, yflux, zflux, kr_ref, pull_ref, zcoef_ref, hcoef_ref,
    out_ref,
    hx_ref, replaced, mask_ref, v1_ref, p_ref, stage, along_z, along_y, *scratch,
):
    x = pl.program_id(0)

    @pl.when(x == 0)
    def _():
        weno_terms(pull_ref, proj, velocity_ref, pressure_ref, speed_ref, kr_ref, scratch)
        hx_ref[...] = jnp.zeros((256, CZ), BF16)
        mask_ref[...] = jnp.zeros((ROWS, 128), F32)
        flat = replaced.reshape(2, VARIABLES * ROWS, 128)
        packed = scratch[-1].reshape(2, VARIABLES * PENCILS, 128)

        def scatter(p, carry):
            row = list_ref[p]
            mask_ref[pl.ds(row, 1), :] = jnp.ones((1, 128), F32)
            for t in range(2):
                for v in range(VARIABLES):
                    flat[t, pl.ds(row + v * ROWS, 1), :] = packed[t, pl.ds(p + v * PENCILS, 1), :]
            return carry

        lax.fori_loop(0, count_ref[0], scatter, 0)

    @pl.when(x > 0)
    def _():
        for part in range(2):
            old = pl.ds(pl.multiple_of(128 * part + 16 * x - 16, 16), 16)
            hx_ref[old, :] = jnp.zeros((16, CZ), BF16)

    for part in range(2):
        new = pl.ds(pl.multiple_of(128 * part + 16 * x, 16), 16)
        hx_ref[new, :] = hcoef_ref[...]

    for t in range(2):
        cut = slice(128 * t, 128 * t + 128)
        velocity1, velocity2, pressure = state_of(lambda v: u_ref[t, v, x])
        v1_ref[t] = velocity1
        p_ref[t] = pressure
        for v in range(VARIABLES):
            high, low = split(flux(u_ref[t, v, x], velocity2, pressure, v, 2))
            stage[v, :, cut] = high
            stage[v, :, 256 + 128 * t : 384 + 128 * t] = low

    rows = VARIABLES * CY
    along_z[...] = dot(
        jnp.concatenate([stage[...].reshape(rows, 512), zflux[...].reshape(rows, 256)], axis=1),
        jnp.concatenate([zcoef_ref[...], zcoef_ref[...], hx_ref[...]], axis=0),
    ).reshape(VARIABLES, CY, CZ)

    hit = mask_ref[pl.ds(pl.multiple_of(CY * x, CY), CY), :] > 0.5
    for v in range(VARIABLES):
        for t in range(2):
            cut = slice(128 * t, 128 * t + 128)
            buffer = along_y.at[v % 2, t]
            value = u_ref[t, v, x]
            buffer[5:8, :] = yflux[0, t, v, pl.ds(3 * x, 3), :]
            buffer[8:72, :] = flux(value, v1_ref[t], p_ref[t], v, 1)
            buffer[72:75, :] = yflux[1, t, v, pl.ds(3 * x, 3), :]

            def at(by):
                return buffer[8 + by : 72 + by, :]

            y_term = 45.0 * (at(1) - at(-1)) - 9.0 * (at(2) - at(-2)) + (at(3) - at(-3))
            z_term = jnp.where(hit, replaced[t, v, x], along_z[v, :, cut])
            out_ref[v, 0, :, cut] = value - SCALE * (y_term + z_term)


def advance(shocked, live_count, prepared, coefs):
    return pl.pallas_call(
        advance_body,
        grid=(CX,),
        out_shape=jax.ShapeDtypeStruct((VARIABLES, CX, CY, CZ), F32),
        in_specs=[SMEM, SMEM] + [VMEM] * 11,
        out_specs=pl.BlockSpec((VARIABLES, 1, CY, CZ), lambda x: (0, x, 0, 0)),
        scratch_shapes=[
            pltpu.VMEM((256, CZ), BF16),
            pltpu.VMEM((2, VARIABLES, CX, CY, 128), F32),
            pltpu.VMEM((ROWS, 128), F32),
            pltpu.VMEM((2, CY, 128), F32),
            pltpu.VMEM((2, CY, 128), F32),
            pltpu.VMEM((VARIABLES, CY, 512), BF16),
            pltpu.VMEM((VARIABLES, CY, CZ), F32),
            pltpu.VMEM((2, 2, 80, 128), F32),
            pltpu.VMEM((CELLS, 128), F32),
            pltpu.VMEM((CELLS, 128), F32),
            pltpu.VMEM((12, CELLS, 128), F32),
            pltpu.VMEM((VARIABLES, CELLS, 128), F32),
            pltpu.VMEM((VARIABLES, CZ, 128), F32),
            pltpu.VMEM((2, VARIABLES, PENCILS, 128), F32),
        ],
        compiler_params=pltpu.CompilerParams(vmem_limit_bytes=36 << 20),
        name="advance",
    )(shocked, live_count, *prepared, *coefs)


@functools.cache
def coefficients():
    weight = {1: 45.0, -1: -45.0, 2: -9.0, -2: 9.0, 3: 1.0, -3: -1.0}

    def coef(offset):
        return weight.get(offset, 0.0)

    zcoef = np.array([[coef(c - k) for k in range(CZ)] for c in range(CZ)])
    cells = [-3, -2, -1, CZ, CZ + 1, CZ + 2]
    hcoef = np.zeros((16, CZ))
    for j, c in enumerate(cells):
        for k in range(CZ):
            hcoef[j, k] = coef(c - k)
    return zcoef, hcoef


def on_device(conserved, char_left, char_right, shock_list, shock_count):
    shocked = shock_list.reshape(PENCILS)
    live_count = shock_count.reshape(1)
    prepared = prepare(shocked, char_left, char_right, conserved)
    coefs = [jnp.asarray(m, BF16) for m in coefficients()]
    return advance(shocked, live_count, prepared, coefs)


def solution(mesh):
    placed = (P(None, "gx", "gy", "gz"), P(), P(), P("gx", "gy", "gz", None), P("gx", "gy", "gz"))
    return jax.shard_map(
        on_device, mesh=mesh, in_specs=placed, out_specs=P(None, "gx", "gy", "gz"), check_vma=False
    )
```

```python
import functools

import jax
import jax.numpy as jnp
import numpy as np
from jax import lax
from jax.experimental import pallas as pl
from jax.experimental.pallas import tpu as pltpu
from jax.sharding import PartitionSpec as P

SPECIES = 9
VARIABLES = 14
CX, CY, CZ = 8, 64, 256
ROWS = CX * CY
PENCILS = 128
GROUP = 16
SIZE = VARIABLES * GROUP
CELLS = 280
TILES = 33
EPS = 0.5e-6
SCALE = 0.2 / 60.0

F32 = jnp.float32
BF16 = jnp.bfloat16
VMEM = pl.BlockSpec(memory_space=pltpu.VMEM)
SMEM = pl.BlockSpec(memory_space=pltpu.SMEM)
HBM = pl.BlockSpec(memory_space=pltpu.HBM)


def lanes(shape):
    return lax.broadcasted_iota(jnp.int32, shape, len(shape) - 1)


def split(values):
    high = values.astype(BF16)
    low = (values - high.astype(F32)).astype(BF16)
    return high, low


def dot(left, right):
    return jnp.dot(left, right, preferred_element_type=F32)


def state_of(read):
    density = read(0)
    for v in range(1, SPECIES):
        density = density + read(v)
    inverse = 1.0 / density
    m0, m1, m2 = read(9), read(10), read(11)
    squares = m0 * m0 + m1 * m1 + m2 * m2
    pressure = 0.4 * (read(12) - read(13) - 0.5 * squares * inverse)
    return m1 * inverse, m2 * inverse, pressure


def flux(value, velocity, pressure, scaled_pressure, v, normal):
    if v == SPECIES + 3:
        return (value + pressure) * velocity
    if v == SPECIES + normal:
        return value * velocity + scaled_pressure
    return value * velocity


def scaled(state):
    velocity1, velocity2, pressure = state
    return SCALE * velocity1, SCALE * velocity2, pressure, SCALE * pressure


def expand(matrix, scale, target):
    row = lax.broadcasted_iota(jnp.int32, (SIZE, SIZE), 0)
    column = lax.broadcasted_iota(jnp.int32, (SIZE, SIZE), 1)
    same = (row & (GROUP - 1)) == (column & (GROUP - 1))
    spread = (
        lax.broadcasted_iota(jnp.int32, (SIZE, VARIABLES), 0) // GROUP
        == lax.broadcasted_iota(jnp.int32, (SIZE, VARIABLES), 1)
    ).astype(BF16)
    gather = (
        lax.broadcasted_iota(jnp.int32, (VARIABLES, SIZE), 1) // GROUP
        == lax.broadcasted_iota(jnp.int32, (VARIABLES, SIZE), 0)
    ).astype(BF16)
    for part, places in zip(split(scale * matrix), ((0, 1), (2,))):
        wide = dot(spread, dot(part, gather).astype(BF16))
        wide = jnp.where(same, wide, 0.0).astype(BF16)
        for place in places:
            target[:, SIZE * place : SIZE * place + SIZE] = wide


def project(matrix, values):
    high, low = split(values)
    return dot(matrix[...], jnp.concatenate([high, low, high], axis=0))


def prepare_body(
    list_ref, where_ref, left_ref, right_ref, u_hbm,
    u_ref, proj, velocity_ref, pressure_ref, speed_ref, yflux, zflux, kr_out, pull_ref,
    rows_ref, cells, kl_ref, up_send, down_send, z_send, y_recv, z_recv,
    load_sems, send_sems, recv_sems,
):
    loads = []

    def load(index, t, x, y):
        copy = pltpu.make_async_copy(
            u_hbm.at[:, x, y, pl.ds(128 * t, 128)], u_ref.at[t, :, x, y], load_sems.at[index]
        )
        copy.start()
        loads.append(copy)

    every = pl.ds(0, CX)
    for t in range(2):
        load(len(loads), t, every, pl.ds(0, 8))
        load(len(loads), t, every, pl.ds(CY - 8, 8))
    for x in range(CX):
        for t in range(2):
            load(len(loads), t, pl.ds(x, 1), pl.ds(8, CY - 16))

    gy, gz = lax.axis_index("gy"), lax.axis_index("gz")
    ny = lax.axis_size("gy")
    above, below = {"gy": lax.rem(gy + 1, ny)}, {"gy": lax.rem(gy + ny - 1, ny)}
    beside = {"gz": 1 - gz}
    barrier = pltpu.get_barrier_semaphore()
    for device in (above, below, beside):
        pl.semaphore_signal(barrier, inc=1, device_id=device, device_id_type=pl.DeviceIdType.MESH)

    def remote(index, source, target, device):
        return pltpu.make_async_remote_copy(
            src_ref=source,
            dst_ref=target,
            send_sem=send_sems.at[index],
            recv_sem=recv_sems.at[index],
            device_id=device,
            device_id_type=pl.DeviceIdType.MESH,
        )

    for copy in loads[:4]:
        copy.wait()

    def y_ends(v, carry):
        for t in range(2):
            for x in range(CX):
                down_send[t, v, 3 * x : 3 * x + 3, :] = u_ref[t, v, x, 0:3, :]
                up_send[t, v, 3 * x : 3 * x + 3, :] = u_ref[t, v, x, CY - 3 : CY, :]
        return carry

    lax.fori_loop(0, VARIABLES, y_ends, 0)
    expand(left_ref[...], 0.5, kl_ref)
    expand(right_ref[...], 0.2, kr_out)
    for k in range(2):
        at = SPECIES + 2 + k
        pull_ref[k, 0:VARIABLES, :] = jnp.broadcast_to(
            0.5 * left_ref[:, at : at + 1], (VARIABLES, 128)
        )
    pl.semaphore_wait(barrier, 3)
    up = remote(0, up_send, y_recv.at[0], above)
    down = remote(1, down_send, y_recv.at[1], below)
    up.start()
    down.start()

    lane = lanes((CY, 128))
    source = lax.broadcasted_iota(jnp.int32, (CX * 128, 128), 0)
    place = lax.broadcasted_iota(jnp.int32, (CX * 128, 128), 1)
    within = ((source & 127) + 3) & 127
    wanted = jnp.minimum(place & 15, 5)
    select = ((place // 16 == source // 128) & (within == wanted)).astype(BF16)
    width = 128 * CX
    for part in range(2):
        some = range(part * CX // 2, (part + 1) * CX // 2)
        for copy in loads[4 + part * CX : 4 + (part + 1) * CX]:
            copy.wait()
        chosen = select[part * width // 2 : (part + 1) * width // 2]
        chosen = jnp.concatenate([chosen, chosen], axis=0)

        def z_ends(v, carry, part=part, some=some, chosen=chosen):
            highs, lows = [], []
            for x in some:
                high, low = split(jnp.where(lane < 64, u_ref[0, v, x], u_ref[1, v, x]))
                highs.append(high)
                lows.append(low)
            packed = dot(jnp.concatenate(highs + lows, axis=1), chosen)
            z_send[v] = packed if part == 0 else z_send[v] + packed
            return carry

        lax.fori_loop(0, VARIABLES, z_ends, 0, unroll=7)

    flat = u_ref.reshape(2, VARIABLES * ROWS, 128)
    packed = rows_ref.reshape(2, VARIABLES * PENCILS, 128)

    def gather(p, carry):
        row = list_ref[p]
        for t in range(2):
            for v in range(VARIABLES):
                packed[t, pl.ds(p + v * PENCILS, 1), :] = flat[t, pl.ds(row + v * ROWS, 1), :]
        return carry

    lax.fori_loop(0, 8, gather, 0, unroll=2)
    ends = remote(2, z_send, z_recv, beside)
    ends.start()
    lax.fori_loop(8, PENCILS, gather, 0, unroll=2)

    def turn(v, carry):
        for t in range(2):
            cells[v, 8 + 128 * t : 136 + 128 * t, :] = rows_ref[t, v].T
        return carry

    lax.fori_loop(0, VARIABLES, turn, 0, unroll=2)

    def wave(i, peak):
        rows = pl.ds(pl.multiple_of(8 * i, 8), 8)
        _, velocity, pressure = state_of(lambda v: cells[v, rows, :])
        velocity_ref[rows, :] = velocity
        pressure_ref[rows, :] = pressure
        return jnp.maximum(peak, jnp.abs(velocity))

    peak = lax.fori_loop(1, 33, wave, jnp.zeros((8, 128), F32), unroll=2)

    def chunk(i, carry):
        first = pl.ds(pl.multiple_of(32 * i + 8, 8), 16)
        second = pl.ds(pl.multiple_of(32 * i + 24, 8), 16)
        values = jnp.concatenate([cells[:, first, :], cells[:, second, :]], axis=-1)
        result = project(kl_ref, values.reshape(SIZE, 256))
        proj[:, first, :] = result[:, 0:128].reshape(VARIABLES, 16, 128)
        proj[:, second, :] = result[:, 128:256].reshape(VARIABLES, 16, 128)
        return carry

    lax.fori_loop(0, CZ // 32, chunk, 0, unroll=4)

    ends.wait()
    halo_rows = z_recv.reshape(VARIABLES * CY, 128)
    fetched = rows_ref.at[0].reshape(VARIABLES * PENCILS, 128)

    def fetch(p, carry):
        y = list_ref[p] % CY
        for v in range(VARIABLES):
            fetched[pl.ds(p + v * PENCILS, 1), :] = halo_rows[pl.ds(y + v * CY, 1), :]
        return carry

    lax.fori_loop(0, PENCILS, fetch, 0, unroll=2)
    own_x = jnp.broadcast_to(where_ref[...] // CY, (16, 128))

    def turn_ends(v, carry):
        turned = rows_ref[0, v].T
        near = turned[0:16]
        for x in range(1, CX):
            near = jnp.where(own_x == x, turned[16 * x : 16 * x + 16], near)
        cells[v, 0:5, :] = near[0:5]
        cells[v, 5:8, :] = near[0:3]
        cells[v, 264:267, :] = near[3:6]
        cells[v, 267:272, :] = near[0:5]
        return carry

    lax.fori_loop(0, VARIABLES, turn_ends, 0, unroll=2)
    peak = wave(0, peak)
    peak = wave(33, peak)
    speed_ref[...] = jnp.broadcast_to(jnp.max(peak, axis=0, keepdims=True) + 1.0, (8, 128))
    values = jnp.concatenate([cells[:, 0:8, :], cells[:, 264:272, :]], axis=1)
    result = project(kl_ref, values.reshape(SIZE, 128)).reshape(VARIABLES, 16, 128)
    proj[:, 0:8, :] = result[:, 0:8]
    proj[:, 264:272, :] = result[:, 8:16]

    _, velocity, pressure, scaled_pressure = scaled(state_of(lambda v: z_recv[v]))
    for v in range(VARIABLES):
        high, low = split(flux(z_recv[v], velocity, pressure, scaled_pressure, v, 2))
        zflux[v, :, 0:128] = high
        zflux[v, :, 128:256] = low

    up.wait()
    down.wait()
    for side in range(2):
        for t in range(2):
            state = scaled(state_of(lambda v: y_recv[side, t, v]))
            for v in range(VARIABLES):
                yflux[side, t, v] = flux(y_recv[side, t, v], state[0], state[2], state[3], v, 1)


def prepare(shocked, left, right, conserved):
    return pl.pallas_call(
        prepare_body,
        out_shape=(
            pltpu.VMEM((2, VARIABLES, CX, CY, 128), F32),
            pltpu.VMEM((VARIABLES, CELLS, 128), F32),
            pltpu.VMEM((CELLS, 128), F32),
            pltpu.VMEM((CELLS, 128), F32),
            pltpu.VMEM((8, 128), F32),
            pltpu.VMEM((2, 2, VARIABLES, 3 * CX, 128), F32),
            pltpu.VMEM((VARIABLES, CY, 256), BF16),
            pltpu.VMEM((SIZE, 3 * SIZE), BF16),
            pltpu.VMEM((2, 16, 128), F32),
        ),
        in_specs=[SMEM, VMEM, VMEM, VMEM, HBM],
        out_specs=(VMEM,) * 9,
        scratch_shapes=[
            pltpu.VMEM((2, VARIABLES, PENCILS, 128), F32),
            pltpu.VMEM((VARIABLES, 272, 128), F32),
            pltpu.VMEM((SIZE, 3 * SIZE), BF16),
            pltpu.VMEM((2, VARIABLES, 3 * CX, 128), F32),
            pltpu.VMEM((2, VARIABLES, 3 * CX, 128), F32),
            pltpu.VMEM((VARIABLES, CY, 128), F32),
            pltpu.VMEM((2, 2, VARIABLES, 3 * CX, 128), F32),
            pltpu.VMEM((VARIABLES, CY, 128), F32),
            pltpu.SemaphoreType.DMA((4 + 2 * CX,)),
            pltpu.SemaphoreType.DMA((3,)),
            pltpu.SemaphoreType.DMA((3,)),
        ],
        compiler_params=pltpu.CompilerParams(
            collective_id=0, has_side_effects=True, vmem_limit_bytes=46 << 20
        ),
        name="prepare",
    )(shocked, shocked.reshape(1, PENCILS), left, right, conserved)


def weno_terms(pull_ref, proj, velocity_ref, pressure_ref, speed_ref, kr_ref, scratch):
    fast_ref, slow_ref, plus_ref, minus_ref, terms, sums, across, terms_out = scratch
    speed = speed_ref[...]

    def sides(i, carry):
        rows = pl.ds(pl.multiple_of(8 * i, 8), 8)
        fast_ref[rows, :] = velocity_ref[rows, :] + speed
        slow_ref[rows, :] = velocity_ref[rows, :] - speed
        return carry

    lax.fori_loop(0, 34, sides, 0, unroll=2)

    def component(v, carry):
        pull = jnp.broadcast_to(pull_ref[0, pl.ds(v, 1), :], (8, 128))
        push = jnp.broadcast_to(pull_ref[1, pl.ds(v, 1), :], (8, 128))

        def fluxes(i, carry):
            rows = pl.ds(pl.multiple_of(8 * i, 8), 8)
            velocity = velocity_ref[rows, :]
            base = proj[v, rows, :]
            source = pressure_ref[rows, :] * (pull + velocity * push)
            plus_ref[rows, :] = fast_ref[rows, :] * base + source
            minus_ref[rows, :] = slow_ref[rows, :] * base + source
            return carry

        lax.fori_loop(0, 34, fluxes, 0, unroll=34)

        def pairs(i, carry):
            row = pl.multiple_of(8 * i, 8)
            for side, source in enumerate((plus_ref, minus_ref)):
                middle = source[pl.ds(row + 6, 8), :]
                x = middle - source[pl.ds(row + 5, 8), :]
                y = source[pl.ds(row + 7, 8), :] - middle
                xx, xy, yy = x * x, x * y, y * y
                shared = (xx + yy) * (2.0 / 3.0) + (EPS - xy * (11.0 / 6.0))
                lean, even, back = 1.0 / (shared + yy), 1.0 / (shared + xy), 1.0 / (shared + xx)
                x2, y2 = x + x, y + y
                if side == 0:
                    w0, w1, w2 = lean * lean, 6.0 * (even * even), 3.0 * (back * back)
                    n0, n1, n2 = 5.0 * y - x2, x + y2, (x2 + x2) - y
                else:
                    w0, w1, w2 = back * back, 6.0 * (even * even), 3.0 * (lean * lean)
                    n0, n1, n2 = 5.0 * x - y2, y + x2, (y2 + y2) - x
                for k, value in enumerate((w0, w1, w2, w0 * n0, w1 * n1, w2 * n2)):
                    terms[6 * side + k, pl.ds(row, 8), :] = value
            return carry

        lax.fori_loop(0, TILES, pairs, 0, unroll=33)

        def faces(i, carry):
            row = pl.multiple_of(8 * i, 8)

            def at(k, by):
                return terms[k, pl.ds(row + by, 8), :]

            gain = (at(3, 0) + at(4, 1) + at(5, 2)) / (at(0, 0) + at(1, 1) + at(2, 2))
            loss = (at(9, 3) + at(10, 2) + at(11, 1)) / (at(6, 3) + at(7, 2) + at(8, 1))
            base = plus_ref[pl.ds(row + 7, 8), :] + minus_ref[pl.ds(row + 8, 8), :]
            sums[v, pl.ds(row, 8), :] = base + (gain - loss) * (1.0 / 6.0)
            return carry

        lax.fori_loop(0, TILES, faces, 0, unroll=33)
        return carry

    lax.fori_loop(0, VARIABLES, component, 0)

    def chunk(i, carry):
        start = pl.multiple_of(32 * i, 8)

        def change(by):
            return sums[:, pl.ds(start + by + 1, 16), :] - sums[:, pl.ds(start + by, 16), :]

        values = jnp.concatenate([change(0), change(16)], axis=-1)
        result = project(kr_ref, values.reshape(SIZE, 256))
        for k in range(2):
            rows = pl.ds(pl.multiple_of(start + 16 * k, 8), 16)
            across[:, rows, :] = result[:, 128 * k : 128 * k + 128].reshape(VARIABLES, 16, 128)
        return carry

    lax.fori_loop(0, CZ // 32, chunk, 0, unroll=4)

    def turn_back(v, carry):
        for t in range(2):
            terms_out[t, v] = across[v, 128 * t : 128 * t + 128, :].T
        return carry

    lax.fori_loop(0, VARIABLES, turn_back, 0, unroll=2)


def advance_body(
    list_ref, count_ref, u_ref,
    proj, velocity_ref, pressure_ref, speed_ref, yflux, zflux, kr_ref, pull_ref, zcoef_ref, hcoef_ref,
    out_ref,
    hx_ref, replaced, mask_ref, v1_ref, p_ref, stage, along_z, along_y, *scratch,
):
    x = pl.program_id(0)

    @pl.when(x == 0)
    def _():
        weno_terms(pull_ref, proj, velocity_ref, pressure_ref, speed_ref, kr_ref, scratch)
        hx_ref[...] = jnp.zeros((256, CZ), BF16)
        mask_ref[...] = jnp.zeros((ROWS, 128), F32)
        flat = replaced.reshape(2, VARIABLES * ROWS, 128)
        packed = scratch[-1].reshape(2, VARIABLES * PENCILS, 128)

        def scatter(p, carry):
            row = list_ref[p]
            mask_ref[pl.ds(row, 1), :] = jnp.ones((1, 128), F32)
            for t in range(2):
                for v in range(VARIABLES):
                    flat[t, pl.ds(row + v * ROWS, 1), :] = packed[t, pl.ds(p + v * PENCILS, 1), :]
            return carry

        lax.fori_loop(0, count_ref[0, 0, 0], scatter, 0)

    @pl.when(x > 0)
    def _():
        for part in range(2):
            old = pl.ds(pl.multiple_of(128 * part + 16 * x - 16, 16), 16)
            hx_ref[old, :] = jnp.zeros((16, CZ), BF16)

    for part in range(2):
        new = pl.ds(pl.multiple_of(128 * part + 16 * x, 16), 16)
        hx_ref[new, :] = hcoef_ref[...]

    for t in range(2):
        cut = slice(128 * t, 128 * t + 128)
        velocity1, velocity2, pressure, scaled_pressure = scaled(
            state_of(lambda v: u_ref[t, v, x])
        )
        v1_ref[t] = velocity1
        p_ref[0, t] = pressure
        p_ref[1, t] = scaled_pressure
        for v in range(VARIABLES):
            high, low = split(flux(u_ref[t, v, x], velocity2, pressure, scaled_pressure, v, 2))
            stage[v, :, cut] = high
            stage[v, :, 256 + 128 * t : 384 + 128 * t] = low

    rows = VARIABLES * CY
    along_z[...] = dot(
        jnp.concatenate([stage[...].reshape(rows, 512), zflux[...].reshape(rows, 256)], axis=1),
        jnp.concatenate([zcoef_ref[...], zcoef_ref[...], hx_ref[...]], axis=0),
    ).reshape(VARIABLES, CY, CZ)

    hit = mask_ref[pl.ds(pl.multiple_of(CY * x, CY), CY), :] > 0.5
    for v in range(VARIABLES):
        for t in range(2):
            cut = slice(128 * t, 128 * t + 128)
            buffer = along_y.at[v % 2, t]
            value = u_ref[t, v, x]
            buffer[5:8, :] = yflux[0, t, v, pl.ds(3 * x, 3), :]
            buffer[8:72, :] = flux(value, v1_ref[t], p_ref[0, t], p_ref[1, t], v, 1)
            buffer[72:75, :] = yflux[1, t, v, pl.ds(3 * x, 3), :]

            def at(by):
                return buffer[8 + by : 72 + by, :]

            y_term = 45.0 * (at(1) - at(-1)) - 9.0 * (at(2) - at(-2)) + (at(3) - at(-3))
            z_term = jnp.where(hit, replaced[t, v, x], along_z[v, :, cut])
            out_ref[v, 0, :, cut] = value - (y_term + z_term)


def advance(shocked, live_count, prepared, coefs):
    return pl.pallas_call(
        advance_body,
        grid=(CX,),
        out_shape=jax.ShapeDtypeStruct((VARIABLES, CX, CY, CZ), F32),
        in_specs=[SMEM, SMEM] + [VMEM] * 11,
        out_specs=pl.BlockSpec((VARIABLES, 1, CY, CZ), lambda x: (0, x, 0, 0)),
        scratch_shapes=[
            pltpu.VMEM((256, CZ), BF16),
            pltpu.VMEM((2, VARIABLES, CX, CY, 128), F32),
            pltpu.VMEM((ROWS, 128), F32),
            pltpu.VMEM((2, CY, 128), F32),
            pltpu.VMEM((2, 2, CY, 128), F32),
            pltpu.VMEM((VARIABLES, CY, 512), BF16),
            pltpu.VMEM((VARIABLES, CY, CZ), F32),
            pltpu.VMEM((2, 2, 80, 128), F32),
            pltpu.VMEM((CELLS, 128), F32),
            pltpu.VMEM((CELLS, 128), F32),
            pltpu.VMEM((CELLS, 128), F32),
            pltpu.VMEM((CELLS, 128), F32),
            pltpu.VMEM((12, CELLS, 128), F32),
            pltpu.VMEM((VARIABLES, CELLS, 128), F32),
            pltpu.VMEM((VARIABLES, CZ, 128), F32),
            pltpu.VMEM((2, VARIABLES, PENCILS, 128), F32),
        ],
        compiler_params=pltpu.CompilerParams(vmem_limit_bytes=36 << 20),
        name="advance",
    )(shocked, live_count, *prepared, *coefs)


@functools.cache
def coefficients():
    weight = {1: 45.0, -1: -45.0, 2: -9.0, -2: 9.0, 3: 1.0, -3: -1.0}

    def coef(offset):
        return weight.get(offset, 0.0)

    zcoef = np.array([[coef(c - k) for k in range(CZ)] for c in range(CZ)])
    cells = [-3, -2, -1, CZ, CZ + 1, CZ + 2]
    hcoef = np.zeros((16, CZ))
    for j, c in enumerate(cells):
        for k in range(CZ):
            hcoef[j, k] = coef(c - k)
    return zcoef, hcoef


def on_device(conserved, char_left, char_right, shock_list, shock_count):
    shocked = shock_list.reshape(PENCILS)
    prepared = prepare(shocked, char_left, char_right, conserved)
    coefs = [jnp.asarray(m, BF16) for m in coefficients()]
    return advance(shocked, shock_count, prepared, coefs)


def solution(mesh):
    placed = (P(None, "gx", "gy", "gz"), P(), P(), P("gx", "gy", "gz", None), P("gx", "gy", "gz"))
    return jax.shard_map(
        on_device, mesh=mesh, in_specs=placed, out_specs=P(None, "gx", "gy", "gz"), check_vma=False
    )
```

```python
import functools

import jax
import jax.numpy as jnp
import numpy as np
from jax import lax
from jax.experimental import pallas as pl
from jax.experimental.pallas import tpu as pltpu
from jax.sharding import PartitionSpec as P

SPECIES = 9
VARIABLES = 14
CX, CY, CZ = 8, 64, 256
ROWS = CX * CY
PENCILS = 128
GROUP = 16
SIZE = VARIABLES * GROUP
CELLS = 280
TILES = 33
EPS = 0.5e-6
SCALE = 0.2 / 60.0

F32 = jnp.float32
BF16 = jnp.bfloat16
VMEM = pl.BlockSpec(memory_space=pltpu.VMEM)
SMEM = pl.BlockSpec(memory_space=pltpu.SMEM)
HBM = pl.BlockSpec(memory_space=pltpu.HBM)


def lanes(shape):
    return lax.broadcasted_iota(jnp.int32, shape, len(shape) - 1)


def split(values):
    high = values.astype(BF16)
    low = (values - high.astype(F32)).astype(BF16)
    return high, low


def dot(left, right):
    return jnp.dot(left, right, preferred_element_type=F32)


def state_of(read):
    density = read(0)
    for v in range(1, SPECIES):
        density = density + read(v)
    inverse = 1.0 / density
    m0, m1, m2 = read(9), read(10), read(11)
    squares = m0 * m0 + m1 * m1 + m2 * m2
    pressure = 0.4 * (read(12) - read(13) - 0.5 * squares * inverse)
    return m1 * inverse, m2 * inverse, pressure


def flux(value, velocity, pressure, scaled_pressure, v, normal):
    if v == SPECIES + 3:
        return (value + pressure) * velocity
    if v == SPECIES + normal:
        return value * velocity + scaled_pressure
    return value * velocity


def scaled(state):
    velocity1, velocity2, pressure = state
    return SCALE * velocity1, SCALE * velocity2, pressure, SCALE * pressure


def expand(matrix, scale, target):
    row = lax.broadcasted_iota(jnp.int32, (SIZE, SIZE), 0)
    column = lax.broadcasted_iota(jnp.int32, (SIZE, SIZE), 1)
    same = (row & (GROUP - 1)) == (column & (GROUP - 1))
    spread = (
        lax.broadcasted_iota(jnp.int32, (SIZE, VARIABLES), 0) // GROUP
        == lax.broadcasted_iota(jnp.int32, (SIZE, VARIABLES), 1)
    ).astype(BF16)
    gather = (
        lax.broadcasted_iota(jnp.int32, (VARIABLES, SIZE), 1) // GROUP
        == lax.broadcasted_iota(jnp.int32, (VARIABLES, SIZE), 0)
    ).astype(BF16)
    for part, places in zip(split(scale * matrix), ((0, 1), (2,))):
        wide = dot(spread, dot(part, gather).astype(BF16))
        wide = jnp.where(same, wide, 0.0).astype(BF16)
        for place in places:
            target[:, SIZE * place : SIZE * place + SIZE] = wide


def project(matrix, values):
    high, low = split(values)
    return dot(matrix[...], jnp.concatenate([high, low, high], axis=0))


def prepare_body(
    list_ref, where_ref, left_ref, right_ref, u_hbm,
    u_ref, proj, velocity_ref, pressure_ref, speed_ref, yflux, zflux, kr_out, pull_ref,
    rows_ref, cells, kl_ref, up_send, down_send, z_send, y_recv, z_recv,
    load_sems, send_sems, recv_sems,
):
    loads = []

    def load(index, t, x, y):
        copy = pltpu.make_async_copy(
            u_hbm.at[:, x, y, pl.ds(128 * t, 128)], u_ref.at[t, :, x, y], load_sems.at[index]
        )
        copy.start()
        loads.append(copy)

    every = pl.ds(0, CX)
    for t in range(2):
        load(len(loads), t, every, pl.ds(0, 8))
        load(len(loads), t, every, pl.ds(CY - 8, 8))
    gy, gz = lax.axis_index("gy"), lax.axis_index("gz")
    ny = lax.axis_size("gy")
    above, below = {"gy": lax.rem(gy + 1, ny)}, {"gy": lax.rem(gy + ny - 1, ny)}
    beside = {"gz": 1 - gz}
    barrier = pltpu.get_barrier_semaphore()
    for device in (above, below, beside):
        pl.semaphore_signal(barrier, inc=1, device_id=device, device_id_type=pl.DeviceIdType.MESH)

    def remote(index, source, target, device):
        return pltpu.make_async_remote_copy(
            src_ref=source,
            dst_ref=target,
            send_sem=send_sems.at[index],
            recv_sem=recv_sems.at[index],
            device_id=device,
            device_id_type=pl.DeviceIdType.MESH,
        )

    for x in range(2):
        for t in range(2):
            load(len(loads), t, pl.ds(x, 1), pl.ds(8, CY - 16))
    for copy in loads[:4]:
        copy.wait()
    for x in range(2, CX):
        for t in range(2):
            load(len(loads), t, pl.ds(x, 1), pl.ds(8, CY - 16))

    def y_ends(v, carry):
        for t in range(2):
            for x in range(CX):
                down_send[t, v, 3 * x : 3 * x + 3, :] = u_ref[t, v, x, 0:3, :]
                up_send[t, v, 3 * x : 3 * x + 3, :] = u_ref[t, v, x, CY - 3 : CY, :]
        return carry

    lax.fori_loop(0, VARIABLES, y_ends, 0)
    expand(left_ref[...], 0.5, kl_ref)
    for k in range(2):
        at = SPECIES + 2 + k
        pull_ref[k, 0:VARIABLES, :] = jnp.broadcast_to(
            0.5 * left_ref[:, at : at + 1], (VARIABLES, 128)
        )
    pl.semaphore_wait(barrier, 3)
    up = remote(0, up_send, y_recv.at[0], above)
    down = remote(1, down_send, y_recv.at[1], below)
    up.start()
    down.start()
    expand(right_ref[...], 0.2, kr_out)

    lane = lanes((CY, 128))
    source = lax.broadcasted_iota(jnp.int32, (CX * 128, 128), 0)
    place = lax.broadcasted_iota(jnp.int32, (CX * 128, 128), 1)
    within = ((source & 127) + 3) & 127
    wanted = jnp.minimum(place & 15, 5)
    select = ((place // 16 == source // 128) & (within == wanted)).astype(BF16)
    width = 128 * CX
    for part in range(2):
        some = range(part * CX // 2, (part + 1) * CX // 2)
        for copy in loads[4 + part * CX : 4 + (part + 1) * CX]:
            copy.wait()
        chosen = select[part * width // 2 : (part + 1) * width // 2]
        chosen = jnp.concatenate([chosen, chosen], axis=0)

        def z_ends(v, carry, part=part, some=some, chosen=chosen):
            highs, lows = [], []
            for x in some:
                high, low = split(jnp.where(lane < 64, u_ref[0, v, x], u_ref[1, v, x]))
                highs.append(high)
                lows.append(low)
            packed = dot(jnp.concatenate(highs + lows, axis=1), chosen)
            z_send[v] = packed if part == 0 else z_send[v] + packed
            return carry

        lax.fori_loop(0, VARIABLES, z_ends, 0, unroll=7)

    flat = u_ref.reshape(2, VARIABLES * ROWS, 128)
    packed = rows_ref.reshape(2, VARIABLES * PENCILS, 128)

    def gather(p, carry):
        row = list_ref[p]
        for t in range(2):
            for v in range(VARIABLES):
                packed[t, pl.ds(p + v * PENCILS, 1), :] = flat[t, pl.ds(row + v * ROWS, 1), :]
        return carry

    lax.fori_loop(0, 8, gather, 0, unroll=2)
    ends = remote(2, z_send, z_recv, beside)
    ends.start()
    lax.fori_loop(8, PENCILS, gather, 0, unroll=2)

    def turn(v, carry):
        for t in range(2):
            cells[v, 8 + 128 * t : 136 + 128 * t, :] = rows_ref[t, v].T
        return carry

    lax.fori_loop(0, VARIABLES, turn, 0, unroll=7)

    def wave(i, peak):
        rows = pl.ds(pl.multiple_of(8 * i, 8), 8)
        _, velocity, pressure = state_of(lambda v: cells[v, rows, :])
        velocity_ref[rows, :] = velocity
        pressure_ref[rows, :] = pressure
        return jnp.maximum(peak, jnp.abs(velocity))

    peak = lax.fori_loop(1, 33, wave, jnp.zeros((8, 128), F32), unroll=2)

    def chunk(i, carry):
        first = pl.ds(pl.multiple_of(32 * i + 8, 8), 16)
        second = pl.ds(pl.multiple_of(32 * i + 24, 8), 16)
        values = jnp.concatenate([cells[:, first, :], cells[:, second, :]], axis=-1)
        result = project(kl_ref, values.reshape(SIZE, 256))
        proj[:, first, :] = result[:, 0:128].reshape(VARIABLES, 16, 128)
        proj[:, second, :] = result[:, 128:256].reshape(VARIABLES, 16, 128)
        return carry

    lax.fori_loop(0, CZ // 32, chunk, 0, unroll=4)

    ends.wait()
    own_y = jnp.broadcast_to(where_ref[...] % CY, (2 * CY, PENCILS))
    pick = own_y == lax.broadcasted_iota(jnp.int32, (2 * CY, PENCILS), 0) % CY
    pick = pick.astype(BF16)
    own_x = jnp.broadcast_to(where_ref[...] // CY, (16, 128))

    def turn_ends(v, carry):
        values = z_recv[v]
        high = values.astype(BF16).astype(F32)
        both = jnp.concatenate([high, values - high], axis=0).T
        turned = dot(both.astype(BF16), pick)
        near = turned[0:16]
        for x in range(1, CX):
            near = jnp.where(own_x == x, turned[16 * x : 16 * x + 16], near)
        cells[v, 0:5, :] = near[0:5]
        cells[v, 5:8, :] = near[0:3]
        cells[v, 264:267, :] = near[3:6]
        cells[v, 267:272, :] = near[0:5]
        return carry

    lax.fori_loop(0, VARIABLES, turn_ends, 0, unroll=7)
    peak = wave(0, peak)
    peak = wave(33, peak)
    speed_ref[...] = jnp.broadcast_to(jnp.max(peak, axis=0, keepdims=True) + 1.0, (8, 128))
    values = jnp.concatenate([cells[:, 0:8, :], cells[:, 264:272, :]], axis=1)
    result = project(kl_ref, values.reshape(SIZE, 128)).reshape(VARIABLES, 16, 128)
    proj[:, 0:8, :] = result[:, 0:8]
    proj[:, 264:272, :] = result[:, 8:16]

    _, velocity, pressure, scaled_pressure = scaled(state_of(lambda v: z_recv[v]))
    for v in range(VARIABLES):
        high, low = split(flux(z_recv[v], velocity, pressure, scaled_pressure, v, 2))
        zflux[v, :, 0:128] = high
        zflux[v, :, 128:256] = low

    up.wait()
    down.wait()
    for side in range(2):
        for t in range(2):
            state = scaled(state_of(lambda v: y_recv[side, t, v]))
            for v in range(VARIABLES):
                yflux[side, t, v] = flux(y_recv[side, t, v], state[0], state[2], state[3], v, 1)


def prepare(shocked, left, right, conserved):
    return pl.pallas_call(
        prepare_body,
        out_shape=(
            pltpu.VMEM((2, VARIABLES, CX, CY, 128), F32),
            pltpu.VMEM((VARIABLES, CELLS, 128), F32),
            pltpu.VMEM((CELLS, 128), F32),
            pltpu.VMEM((CELLS, 128), F32),
            pltpu.VMEM((8, 128), F32),
            pltpu.VMEM((2, 2, VARIABLES, 3 * CX, 128), F32),
            pltpu.VMEM((VARIABLES, CY, 256), BF16),
            pltpu.VMEM((SIZE, 3 * SIZE), BF16),
            pltpu.VMEM((2, 16, 128), F32),
        ),
        in_specs=[SMEM, VMEM, VMEM, VMEM, HBM],
        out_specs=(VMEM,) * 9,
        scratch_shapes=[
            pltpu.VMEM((2, VARIABLES, PENCILS, 128), F32),
            pltpu.VMEM((VARIABLES, 272, 128), F32),
            pltpu.VMEM((SIZE, 3 * SIZE), BF16),
            pltpu.VMEM((2, VARIABLES, 3 * CX, 128), F32),
            pltpu.VMEM((2, VARIABLES, 3 * CX, 128), F32),
            pltpu.VMEM((VARIABLES, CY, 128), F32),
            pltpu.VMEM((2, 2, VARIABLES, 3 * CX, 128), F32),
            pltpu.VMEM((VARIABLES, CY, 128), F32),
            pltpu.SemaphoreType.DMA((4 + 2 * CX,)),
            pltpu.SemaphoreType.DMA((3,)),
            pltpu.SemaphoreType.DMA((3,)),
        ],
        compiler_params=pltpu.CompilerParams(
            collective_id=0, has_side_effects=True, vmem_limit_bytes=46 << 20
        ),
        name="prepare",
    )(shocked, shocked.reshape(1, PENCILS), left, right, conserved)


def weno_terms(pull_ref, proj, velocity_ref, pressure_ref, speed_ref, kr_ref, scratch):
    fast_ref, slow_ref, plus_ref, minus_ref, terms, sums, across, terms_out = scratch
    speed = speed_ref[...]

    def sides(i, carry):
        rows = pl.ds(pl.multiple_of(8 * i, 8), 8)
        fast_ref[rows, :] = velocity_ref[rows, :] + speed
        slow_ref[rows, :] = velocity_ref[rows, :] - speed
        return carry

    lax.fori_loop(0, 34, sides, 0, unroll=2)

    def component(v, carry):
        pull = jnp.broadcast_to(pull_ref[0, pl.ds(v, 1), :], (8, 128))
        push = jnp.broadcast_to(pull_ref[1, pl.ds(v, 1), :], (8, 128))

        def fluxes(i, carry):
            rows = pl.ds(pl.multiple_of(8 * i, 8), 8)
            velocity = velocity_ref[rows, :]
            base = proj[v, rows, :]
            source = pressure_ref[rows, :] * (pull + velocity * push)
            plus_ref[rows, :] = fast_ref[rows, :] * base + source
            minus_ref[rows, :] = slow_ref[rows, :] * base + source
            return carry

        lax.fori_loop(0, 34, fluxes, 0, unroll=34)

        def pairs(i, carry):
            row = pl.multiple_of(8 * i, 8)
            for side, source in enumerate((plus_ref, minus_ref)):
                middle = source[pl.ds(row + 6, 8), :]
                x = middle - source[pl.ds(row + 5, 8), :]
                y = source[pl.ds(row + 7, 8), :] - middle
                xx, xy, yy = x * x, x * y, y * y
                shared = (xx + yy) * (2.0 / 3.0) + (EPS - xy * (11.0 / 6.0))
                lean, even, back = 1.0 / (shared + yy), 1.0 / (shared + xy), 1.0 / (shared + xx)
                x2, y2 = x + x, y + y
                if side == 0:
                    w0, w1, w2 = lean * lean, 6.0 * (even * even), 3.0 * (back * back)
                    n0, n1, n2 = 5.0 * y - x2, x + y2, (x2 + x2) - y
                else:
                    w0, w1, w2 = back * back, 6.0 * (even * even), 3.0 * (lean * lean)
                    n0, n1, n2 = 5.0 * x - y2, y + x2, (y2 + y2) - x
                for k, value in enumerate((w0, w1, w2, w0 * n0, w1 * n1, w2 * n2)):
                    terms[6 * side + k, pl.ds(row, 8), :] = value
            return carry

        lax.fori_loop(0, TILES, pairs, 0, unroll=33)

        def faces(i, carry):
            row = pl.multiple_of(8 * i, 8)

            def at(k, by):
                return terms[k, pl.ds(row + by, 8), :]

            gain = (at(3, 0) + at(4, 1) + at(5, 2)) / (at(0, 0) + at(1, 1) + at(2, 2))
            loss = (at(9, 3) + at(10, 2) + at(11, 1)) / (at(6, 3) + at(7, 2) + at(8, 1))
            base = plus_ref[pl.ds(row + 7, 8), :] + minus_ref[pl.ds(row + 8, 8), :]
            sums[v, pl.ds(row, 8), :] = base + (gain - loss) * (1.0 / 6.0)
            return carry

        lax.fori_loop(0, TILES, faces, 0, unroll=33)
        return carry

    lax.fori_loop(0, VARIABLES, component, 0)

    def chunk(i, carry):
        start = pl.multiple_of(32 * i, 8)

        def change(by):
            return sums[:, pl.ds(start + by + 1, 16), :] - sums[:, pl.ds(start + by, 16), :]

        values = jnp.concatenate([change(0), change(16)], axis=-1)
        result = project(kr_ref, values.reshape(SIZE, 256))
        for k in range(2):
            rows = pl.ds(pl.multiple_of(start + 16 * k, 8), 16)
            across[:, rows, :] = result[:, 128 * k : 128 * k + 128].reshape(VARIABLES, 16, 128)
        return carry

    lax.fori_loop(0, CZ // 32, chunk, 0, unroll=4)

    def turn_back(v, carry):
        for t in range(2):
            terms_out[t, v] = across[v, 128 * t : 128 * t + 128, :].T
        return carry

    lax.fori_loop(0, VARIABLES, turn_back, 0, unroll=2)


def advance_body(
    list_ref, count_ref, u_ref,
    proj, velocity_ref, pressure_ref, speed_ref, yflux, zflux, kr_ref, pull_ref, zcoef_ref, hcoef_ref,
    out_ref,
    hx_ref, replaced, mask_ref, v1_ref, p_ref, stage, along_z, along_y, *scratch,
):
    x = pl.program_id(0)

    @pl.when(x == 0)
    def _():
        weno_terms(pull_ref, proj, velocity_ref, pressure_ref, speed_ref, kr_ref, scratch)
        hx_ref[...] = jnp.zeros((256, CZ), BF16)
        mask_ref[...] = jnp.zeros((ROWS, 128), F32)
        flat = replaced.reshape(2, VARIABLES * ROWS, 128)
        packed = scratch[-1].reshape(2, VARIABLES * PENCILS, 128)

        def scatter(p, carry):
            row = list_ref[p]
            mask_ref[pl.ds(row, 1), :] = jnp.ones((1, 128), F32)
            for t in range(2):
                for v in range(VARIABLES):
                    flat[t, pl.ds(row + v * ROWS, 1), :] = packed[t, pl.ds(p + v * PENCILS, 1), :]
            return carry

        lax.fori_loop(0, count_ref[0, 0, 0], scatter, 0)

    @pl.when(x > 0)
    def _():
        for part in range(2):
            old = pl.ds(pl.multiple_of(128 * part + 16 * x - 16, 16), 16)
            hx_ref[old, :] = jnp.zeros((16, CZ), BF16)

    for part in range(2):
        new = pl.ds(pl.multiple_of(128 * part + 16 * x, 16), 16)
        hx_ref[new, :] = hcoef_ref[...]

    for t in range(2):
        cut = slice(128 * t, 128 * t + 128)
        velocity1, velocity2, pressure, scaled_pressure = scaled(
            state_of(lambda v: u_ref[t, v, x])
        )
        v1_ref[t] = velocity1
        p_ref[0, t] = pressure
        p_ref[1, t] = scaled_pressure
        for v in range(VARIABLES):
            high, low = split(flux(u_ref[t, v, x], velocity2, pressure, scaled_pressure, v, 2))
            stage[v, :, cut] = high
            stage[v, :, 256 + 128 * t : 384 + 128 * t] = low

    rows = VARIABLES * CY
    along_z[...] = dot(
        jnp.concatenate([stage[...].reshape(rows, 512), zflux[...].reshape(rows, 256)], axis=1),
        jnp.concatenate([zcoef_ref[...], zcoef_ref[...], hx_ref[...]], axis=0),
    ).reshape(VARIABLES, CY, CZ)

    hit = mask_ref[pl.ds(pl.multiple_of(CY * x, CY), CY), :] > 0.5
    for v in range(VARIABLES):
        for t in range(2):
            cut = slice(128 * t, 128 * t + 128)
            buffer = along_y.at[v % 2, t]
            value = u_ref[t, v, x]
            buffer[5:8, :] = yflux[0, t, v, pl.ds(3 * x, 3), :]
            buffer[8:72, :] = flux(value, v1_ref[t], p_ref[0, t], p_ref[1, t], v, 1)
            buffer[72:75, :] = yflux[1, t, v, pl.ds(3 * x, 3), :]

            def at(by):
                return buffer[8 + by : 72 + by, :]

            y_term = 45.0 * (at(1) - at(-1)) - 9.0 * (at(2) - at(-2)) + (at(3) - at(-3))
            z_term = jnp.where(hit, replaced[t, v, x], along_z[v, :, cut])
            out_ref[v, 0, :, cut] = value - (y_term + z_term)


def advance(shocked, live_count, prepared, coefs):
    return pl.pallas_call(
        advance_body,
        grid=(CX,),
        out_shape=jax.ShapeDtypeStruct((VARIABLES, CX, CY, CZ), F32),
        in_specs=[SMEM, SMEM] + [VMEM] * 11,
        out_specs=pl.BlockSpec((VARIABLES, 1, CY, CZ), lambda x: (0, x, 0, 0)),
        scratch_shapes=[
            pltpu.VMEM((256, CZ), BF16),
            pltpu.VMEM((2, VARIABLES, CX, CY, 128), F32),
            pltpu.VMEM((ROWS, 128), F32),
            pltpu.VMEM((2, CY, 128), F32),
            pltpu.VMEM((2, 2, CY, 128), F32),
            pltpu.VMEM((VARIABLES, CY, 512), BF16),
            pltpu.VMEM((VARIABLES, CY, CZ), F32),
            pltpu.VMEM((2, 2, 80, 128), F32),
            pltpu.VMEM((CELLS, 128), F32),
            pltpu.VMEM((CELLS, 128), F32),
            pltpu.VMEM((CELLS, 128), F32),
            pltpu.VMEM((CELLS, 128), F32),
            pltpu.VMEM((12, CELLS, 128), F32),
            pltpu.VMEM((VARIABLES, CELLS, 128), F32),
            pltpu.VMEM((VARIABLES, CZ, 128), F32),
            pltpu.VMEM((2, VARIABLES, PENCILS, 128), F32),
        ],
        compiler_params=pltpu.CompilerParams(vmem_limit_bytes=36 << 20),
        name="advance",
    )(shocked, live_count, *prepared, *coefs)


@functools.cache
def coefficients():
    weight = {1: 45.0, -1: -45.0, 2: -9.0, -2: 9.0, 3: 1.0, -3: -1.0}

    def coef(offset):
        return weight.get(offset, 0.0)

    zcoef = np.array([[coef(c - k) for k in range(CZ)] for c in range(CZ)])
    cells = [-3, -2, -1, CZ, CZ + 1, CZ + 2]
    hcoef = np.zeros((16, CZ))
    for j, c in enumerate(cells):
        for k in range(CZ):
            hcoef[j, k] = coef(c - k)
    return zcoef, hcoef


def on_device(conserved, char_left, char_right, shock_list, shock_count):
    shocked = shock_list.reshape(PENCILS)
    prepared = prepare(shocked, char_left, char_right, conserved)
    coefs = [jnp.asarray(m, BF16) for m in coefficients()]
    return advance(shocked, shock_count, prepared, coefs)


def solution(mesh):
    placed = (P(None, "gx", "gy", "gz"), P(), P(), P("gx", "gy", "gz", None), P("gx", "gy", "gz"))
    return jax.shard_map(
        on_device, mesh=mesh, in_specs=placed, out_specs=P(None, "gx", "gy", "gz"), check_vma=False
    )
```

```python
import functools

import jax
import jax.numpy as jnp
import numpy as np
from jax import lax
from jax.experimental import pallas as pl
from jax.experimental.pallas import tpu as pltpu
from jax.sharding import PartitionSpec as P

SPECIES = 9
VARIABLES = 14
CX, CY, CZ = 8, 64, 256
ROWS = CX * CY
PENCILS = 128
GROUP = 16
SIZE = VARIABLES * GROUP
CELLS = 280
TILES = 33
EPS = 0.5e-6
SCALE = 0.2 / 60.0

F32 = jnp.float32
BF16 = jnp.bfloat16
VMEM = pl.BlockSpec(memory_space=pltpu.VMEM)
SMEM = pl.BlockSpec(memory_space=pltpu.SMEM)
HBM = pl.BlockSpec(memory_space=pltpu.HBM)


def lanes(shape):
    return lax.broadcasted_iota(jnp.int32, shape, len(shape) - 1)


def split(values):
    high = values.astype(BF16)
    low = (values - high.astype(F32)).astype(BF16)
    return high, low


def dot(left, right):
    return jnp.dot(left, right, preferred_element_type=F32)


def state_of(read):
    density = read(0)
    for v in range(1, SPECIES):
        density = density + read(v)
    inverse = 1.0 / density
    m0, m1, m2 = read(9), read(10), read(11)
    squares = m0 * m0 + m1 * m1 + m2 * m2
    pressure = 0.4 * (read(12) - read(13) - 0.5 * squares * inverse)
    return m1 * inverse, m2 * inverse, pressure


def flux(value, velocity, pressure, scaled_pressure, v, normal):
    if v == SPECIES + 3:
        return (value + pressure) * velocity
    if v == SPECIES + normal:
        return value * velocity + scaled_pressure
    return value * velocity


def scaled(state):
    velocity1, velocity2, pressure = state
    return SCALE * velocity1, SCALE * velocity2, pressure, SCALE * pressure


def expand(matrix, scale, target):
    row = lax.broadcasted_iota(jnp.int32, (SIZE, SIZE), 0)
    column = lax.broadcasted_iota(jnp.int32, (SIZE, SIZE), 1)
    same = (row & (GROUP - 1)) == (column & (GROUP - 1))
    spread = (
        lax.broadcasted_iota(jnp.int32, (SIZE, VARIABLES), 0) // GROUP
        == lax.broadcasted_iota(jnp.int32, (SIZE, VARIABLES), 1)
    ).astype(BF16)
    gather = (
        lax.broadcasted_iota(jnp.int32, (VARIABLES, SIZE), 1) // GROUP
        == lax.broadcasted_iota(jnp.int32, (VARIABLES, SIZE), 0)
    ).astype(BF16)
    for part, places in zip(split(scale * matrix), ((0, 1), (2,))):
        wide = dot(spread, dot(part, gather).astype(BF16))
        wide = jnp.where(same, wide, 0.0).astype(BF16)
        for place in places:
            target[:, SIZE * place : SIZE * place + SIZE] = wide


def project(matrix, values):
    high, low = split(values)
    return dot(matrix[...], jnp.concatenate([high, low, high], axis=0))


def face_sums(speed, pull_ref, proj, velocity_ref, pressure_ref, scratch, sums):
    fast_ref, slow_ref, plus_ref, minus_ref, terms = scratch

    def sides(i, carry):
        rows = pl.ds(pl.multiple_of(8 * i, 8), 8)
        fast_ref[rows, :] = velocity_ref[rows, :] + speed
        slow_ref[rows, :] = velocity_ref[rows, :] - speed
        return carry

    lax.fori_loop(0, 34, sides, 0, unroll=2)

    def component(v, carry):
        pull = jnp.broadcast_to(pull_ref[0, pl.ds(v, 1), :], (8, 128))
        push = jnp.broadcast_to(pull_ref[1, pl.ds(v, 1), :], (8, 128))

        def fluxes(i, carry):
            rows = pl.ds(pl.multiple_of(8 * i, 8), 8)
            velocity = velocity_ref[rows, :]
            base = proj[v, rows, :]
            source = pressure_ref[rows, :] * (pull + velocity * push)
            plus_ref[rows, :] = fast_ref[rows, :] * base + source
            minus_ref[rows, :] = slow_ref[rows, :] * base + source
            return carry

        lax.fori_loop(0, 34, fluxes, 0, unroll=34)

        def pairs(i, carry):
            row = pl.multiple_of(8 * i, 8)
            for side, source in enumerate((plus_ref, minus_ref)):
                middle = source[pl.ds(row + 6, 8), :]
                x = middle - source[pl.ds(row + 5, 8), :]
                y = source[pl.ds(row + 7, 8), :] - middle
                xx, xy, yy = x * x, x * y, y * y
                shared = (xx + yy) * (2.0 / 3.0) + (EPS - xy * (11.0 / 6.0))
                lean, even, back = 1.0 / (shared + yy), 1.0 / (shared + xy), 1.0 / (shared + xx)
                x2, y2 = x + x, y + y
                if side == 0:
                    w0, w1, w2 = lean * lean, 6.0 * (even * even), 3.0 * (back * back)
                    n0, n1, n2 = 5.0 * y - x2, x + y2, (x2 + x2) - y
                else:
                    w0, w1, w2 = back * back, 6.0 * (even * even), 3.0 * (lean * lean)
                    n0, n1, n2 = 5.0 * x - y2, y + x2, (y2 + y2) - x
                for k, value in enumerate((w0, w1, w2, w0 * n0, w1 * n1, w2 * n2)):
                    terms[6 * side + k, pl.ds(row, 8), :] = value
            return carry

        lax.fori_loop(0, TILES, pairs, 0, unroll=33)

        def faces(i, carry):
            row = pl.multiple_of(8 * i, 8)

            def at(k, by):
                return terms[k, pl.ds(row + by, 8), :]

            gain = (at(3, 0) + at(4, 1) + at(5, 2)) / (at(0, 0) + at(1, 1) + at(2, 2))
            loss = (at(9, 3) + at(10, 2) + at(11, 1)) / (at(6, 3) + at(7, 2) + at(8, 1))
            base = plus_ref[pl.ds(row + 7, 8), :] + minus_ref[pl.ds(row + 8, 8), :]
            sums[v, pl.ds(row, 8), :] = base + (gain - loss) * (1.0 / 6.0)
            return carry

        lax.fori_loop(0, TILES, faces, 0, unroll=33)
        return carry

    lax.fori_loop(0, VARIABLES, component, 0)


def prepare_body(
    list_ref, where_ref, left_ref, right_ref, u_hbm,
    u_ref, sums, yflux, zflux, kr_out,
    proj, velocity_ref, pressure_ref, pull_ref,
    rows_ref, cells, kl_ref, up_send, down_send, z_send, y_recv, z_recv,
    load_sems, send_sems, recv_sems, *scratch,
):
    loads = []

    def load(index, t, x, y):
        copy = pltpu.make_async_copy(
            u_hbm.at[:, x, y, pl.ds(128 * t, 128)], u_ref.at[t, :, x, y], load_sems.at[index]
        )
        copy.start()
        loads.append(copy)

    every = pl.ds(0, CX)
    for t in range(2):
        load(len(loads), t, every, pl.ds(0, 8))
        load(len(loads), t, every, pl.ds(CY - 8, 8))
    gy, gz = lax.axis_index("gy"), lax.axis_index("gz")
    ny = lax.axis_size("gy")
    above, below = {"gy": lax.rem(gy + 1, ny)}, {"gy": lax.rem(gy + ny - 1, ny)}
    beside = {"gz": 1 - gz}
    barrier = pltpu.get_barrier_semaphore()
    for device in (above, below, beside):
        pl.semaphore_signal(barrier, inc=1, device_id=device, device_id_type=pl.DeviceIdType.MESH)

    def remote(index, source, target, device):
        return pltpu.make_async_remote_copy(
            src_ref=source,
            dst_ref=target,
            send_sem=send_sems.at[index],
            recv_sem=recv_sems.at[index],
            device_id=device,
            device_id_type=pl.DeviceIdType.MESH,
        )

    for x in range(2):
        for t in range(2):
            load(len(loads), t, pl.ds(x, 1), pl.ds(8, CY - 16))
    for copy in loads[:4]:
        copy.wait()
    for x in range(2, CX):
        for t in range(2):
            load(len(loads), t, pl.ds(x, 1), pl.ds(8, CY - 16))

    def y_ends(v, carry):
        for t in range(2):
            for x in range(CX):
                down_send[t, v, 3 * x : 3 * x + 3, :] = u_ref[t, v, x, 0:3, :]
                up_send[t, v, 3 * x : 3 * x + 3, :] = u_ref[t, v, x, CY - 3 : CY, :]
        return carry

    lax.fori_loop(0, VARIABLES, y_ends, 0)
    expand(left_ref[...], 0.5, kl_ref)
    for k in range(2):
        at = SPECIES + 2 + k
        pull_ref[k, 0:VARIABLES, :] = jnp.broadcast_to(
            0.5 * left_ref[:, at : at + 1], (VARIABLES, 128)
        )
    pl.semaphore_wait(barrier, 3)
    up = remote(0, up_send, y_recv.at[0], above)
    down = remote(1, down_send, y_recv.at[1], below)
    up.start()
    down.start()
    expand(right_ref[...], 0.2, kr_out)

    lane = lanes((CY, 128))
    source = lax.broadcasted_iota(jnp.int32, (CX * 128, 128), 0)
    place = lax.broadcasted_iota(jnp.int32, (CX * 128, 128), 1)
    within = ((source & 127) + 3) & 127
    wanted = jnp.minimum(place & 15, 5)
    select = ((place // 16 == source // 128) & (within == wanted)).astype(BF16)
    width = 128 * CX
    for part in range(2):
        some = range(part * CX // 2, (part + 1) * CX // 2)
        for copy in loads[4 + part * CX : 4 + (part + 1) * CX]:
            copy.wait()
        chosen = select[part * width // 2 : (part + 1) * width // 2]
        chosen = jnp.concatenate([chosen, chosen], axis=0)

        def z_ends(v, carry, part=part, some=some, chosen=chosen):
            highs, lows = [], []
            for x in some:
                high, low = split(jnp.where(lane < 64, u_ref[0, v, x], u_ref[1, v, x]))
                highs.append(high)
                lows.append(low)
            packed = dot(jnp.concatenate(highs + lows, axis=1), chosen)
            z_send[v] = packed if part == 0 else z_send[v] + packed
            return carry

        lax.fori_loop(0, VARIABLES, z_ends, 0, unroll=7)

    flat = u_ref.reshape(2, VARIABLES * ROWS, 128)
    packed = rows_ref.reshape(2, VARIABLES * PENCILS, 128)

    def gather(p, carry):
        row = list_ref[p]
        for t in range(2):
            for v in range(VARIABLES):
                packed[t, pl.ds(p + v * PENCILS, 1), :] = flat[t, pl.ds(row + v * ROWS, 1), :]
        return carry

    lax.fori_loop(0, 8, gather, 0, unroll=2)
    ends = remote(2, z_send, z_recv, beside)
    ends.start()
    lax.fori_loop(8, PENCILS, gather, 0, unroll=2)

    def turn(v, carry):
        for t in range(2):
            cells[v, 8 + 128 * t : 136 + 128 * t, :] = rows_ref[t, v].T
        return carry

    lax.fori_loop(0, VARIABLES, turn, 0, unroll=7)

    def wave(i, peak):
        rows = pl.ds(pl.multiple_of(8 * i, 8), 8)
        _, velocity, pressure = state_of(lambda v: cells[v, rows, :])
        velocity_ref[rows, :] = velocity
        pressure_ref[rows, :] = pressure
        return jnp.maximum(peak, jnp.abs(velocity))

    peak = lax.fori_loop(1, 33, wave, jnp.zeros((8, 128), F32), unroll=2)

    def chunk(i, carry):
        first = pl.ds(pl.multiple_of(32 * i + 8, 8), 16)
        second = pl.ds(pl.multiple_of(32 * i + 24, 8), 16)
        values = jnp.concatenate([cells[:, first, :], cells[:, second, :]], axis=-1)
        result = project(kl_ref, values.reshape(SIZE, 256))
        proj[:, first, :] = result[:, 0:128].reshape(VARIABLES, 16, 128)
        proj[:, second, :] = result[:, 128:256].reshape(VARIABLES, 16, 128)
        return carry

    lax.fori_loop(0, CZ // 32, chunk, 0, unroll=4)

    ends.wait()
    own_y = jnp.broadcast_to(where_ref[...] % CY, (2 * CY, PENCILS))
    pick = own_y == lax.broadcasted_iota(jnp.int32, (2 * CY, PENCILS), 0) % CY
    pick = pick.astype(BF16)
    own_x = jnp.broadcast_to(where_ref[...] // CY, (16, 128))

    def turn_ends(v, carry):
        values = z_recv[v]
        high = values.astype(BF16).astype(F32)
        both = jnp.concatenate([high, values - high], axis=0).T
        turned = dot(both.astype(BF16), pick)
        near = turned[0:16]
        for x in range(1, CX):
            near = jnp.where(own_x == x, turned[16 * x : 16 * x + 16], near)
        cells[v, 0:5, :] = near[0:5]
        cells[v, 5:8, :] = near[0:3]
        cells[v, 264:267, :] = near[3:6]
        cells[v, 267:272, :] = near[0:5]
        return carry

    lax.fori_loop(0, VARIABLES, turn_ends, 0, unroll=7)
    peak = wave(0, peak)
    peak = wave(33, peak)
    speed = jnp.broadcast_to(jnp.max(peak, axis=0, keepdims=True) + 1.0, (8, 128))
    values = jnp.concatenate([cells[:, 0:8, :], cells[:, 264:272, :]], axis=1)
    result = project(kl_ref, values.reshape(SIZE, 128)).reshape(VARIABLES, 16, 128)
    proj[:, 0:8, :] = result[:, 0:8]
    proj[:, 264:272, :] = result[:, 8:16]

    _, velocity, pressure, scaled_pressure = scaled(state_of(lambda v: z_recv[v]))
    for v in range(VARIABLES):
        high, low = split(flux(z_recv[v], velocity, pressure, scaled_pressure, v, 2))
        zflux[v, :, 0:128] = high
        zflux[v, :, 128:256] = low

    face_sums(speed, pull_ref, proj, velocity_ref, pressure_ref, scratch, sums)

    up.wait()
    down.wait()
    for side in range(2):
        for t in range(2):
            state = scaled(state_of(lambda v: y_recv[side, t, v]))
            for v in range(VARIABLES):
                yflux[side, t, v] = flux(y_recv[side, t, v], state[0], state[2], state[3], v, 1)


def prepare(shocked, left, right, conserved):
    return pl.pallas_call(
        prepare_body,
        out_shape=(
            pltpu.VMEM((2, VARIABLES, CX, CY, 128), F32),
            pltpu.VMEM((VARIABLES, CELLS, 128), F32),
            pltpu.VMEM((2, 2, VARIABLES, 3 * CX, 128), F32),
            pltpu.VMEM((VARIABLES, CY, 256), BF16),
            pltpu.VMEM((SIZE, 3 * SIZE), BF16),
        ),
        in_specs=[SMEM, VMEM, VMEM, VMEM, HBM],
        out_specs=(VMEM,) * 5,
        scratch_shapes=[
            pltpu.VMEM((VARIABLES, CELLS, 128), F32),
            pltpu.VMEM((CELLS, 128), F32),
            pltpu.VMEM((CELLS, 128), F32),
            pltpu.VMEM((2, 16, 128), F32),
            pltpu.VMEM((2, VARIABLES, PENCILS, 128), F32),
            pltpu.VMEM((VARIABLES, 272, 128), F32),
            pltpu.VMEM((SIZE, 3 * SIZE), BF16),
            pltpu.VMEM((2, VARIABLES, 3 * CX, 128), F32),
            pltpu.VMEM((2, VARIABLES, 3 * CX, 128), F32),
            pltpu.VMEM((VARIABLES, CY, 128), F32),
            pltpu.VMEM((2, 2, VARIABLES, 3 * CX, 128), F32),
            pltpu.VMEM((VARIABLES, CY, 128), F32),
            pltpu.SemaphoreType.DMA((4 + 2 * CX,)),
            pltpu.SemaphoreType.DMA((3,)),
            pltpu.SemaphoreType.DMA((3,)),
            pltpu.VMEM((CELLS, 128), F32),
            pltpu.VMEM((CELLS, 128), F32),
            pltpu.VMEM((CELLS, 128), F32),
            pltpu.VMEM((CELLS, 128), F32),
            pltpu.VMEM((12, CELLS, 128), F32),
        ],
        compiler_params=pltpu.CompilerParams(
            collective_id=0, has_side_effects=True, vmem_limit_bytes=46 << 20
        ),
        name="prepare",
    )(shocked, shocked.reshape(1, PENCILS), left, right, conserved)


def weno_terms(sums, kr_ref, across, terms_out):
    def chunk(i, carry):
        start = pl.multiple_of(32 * i, 8)

        def change(by):
            return sums[:, pl.ds(start + by + 1, 16), :] - sums[:, pl.ds(start + by, 16), :]

        values = jnp.concatenate([change(0), change(16)], axis=-1)
        result = project(kr_ref, values.reshape(SIZE, 256))
        for k in range(2):
            rows = pl.ds(pl.multiple_of(start + 16 * k, 8), 16)
            across[:, rows, :] = result[:, 128 * k : 128 * k + 128].reshape(VARIABLES, 16, 128)
        return carry

    lax.fori_loop(0, CZ // 32, chunk, 0, unroll=4)

    def turn_back(v, carry):
        for t in range(2):
            terms_out[t, v] = across[v, 128 * t : 128 * t + 128, :].T
        return carry

    lax.fori_loop(0, VARIABLES, turn_back, 0, unroll=2)


def advance_body(
    list_ref, count_ref, u_ref,
    sums, yflux, zflux, kr_ref, zcoef_ref, hcoef_ref,
    out_ref,
    hx_ref, replaced, mask_ref, v1_ref, p_ref, stage, along_z, along_y, across, terms_out,
):
    x = pl.program_id(0)

    @pl.when(x == 0)
    def _():
        weno_terms(sums, kr_ref, across, terms_out)
        hx_ref[...] = jnp.zeros((256, CZ), BF16)
        mask_ref[...] = jnp.zeros((ROWS, 128), F32)
        flat = replaced.reshape(2, VARIABLES * ROWS, 128)
        packed = terms_out.reshape(2, VARIABLES * PENCILS, 128)

        def scatter(p, carry):
            row = list_ref[p]
            mask_ref[pl.ds(row, 1), :] = jnp.ones((1, 128), F32)
            for t in range(2):
                for v in range(VARIABLES):
                    flat[t, pl.ds(row + v * ROWS, 1), :] = packed[t, pl.ds(p + v * PENCILS, 1), :]
            return carry

        lax.fori_loop(0, count_ref[0, 0, 0], scatter, 0)

    @pl.when(x > 0)
    def _():
        for part in range(2):
            old = pl.ds(pl.multiple_of(128 * part + 16 * x - 16, 16), 16)
            hx_ref[old, :] = jnp.zeros((16, CZ), BF16)

    for part in range(2):
        new = pl.ds(pl.multiple_of(128 * part + 16 * x, 16), 16)
        hx_ref[new, :] = hcoef_ref[...]

    for t in range(2):
        cut = slice(128 * t, 128 * t + 128)
        velocity1, velocity2, pressure, scaled_pressure = scaled(
            state_of(lambda v: u_ref[t, v, x])
        )
        v1_ref[t] = velocity1
        p_ref[0, t] = pressure
        p_ref[1, t] = scaled_pressure
        for v in range(VARIABLES):
            high, low = split(flux(u_ref[t, v, x], velocity2, pressure, scaled_pressure, v, 2))
            stage[v, :, cut] = high
            stage[v, :, 256 + 128 * t : 384 + 128 * t] = low

    rows = VARIABLES * CY
    along_z[...] = dot(
        jnp.concatenate([stage[...].reshape(rows, 512), zflux[...].reshape(rows, 256)], axis=1),
        jnp.concatenate([zcoef_ref[...], zcoef_ref[...], hx_ref[...]], axis=0),
    ).reshape(VARIABLES, CY, CZ)

    hit = mask_ref[pl.ds(pl.multiple_of(CY * x, CY), CY), :] > 0.5
    for v in range(VARIABLES):
        for t in range(2):
            cut = slice(128 * t, 128 * t + 128)
            buffer = along_y.at[v % 2, t]
            value = u_ref[t, v, x]
            buffer[5:8, :] = yflux[0, t, v, pl.ds(3 * x, 3), :]
            buffer[8:72, :] = flux(value, v1_ref[t], p_ref[0, t], p_ref[1, t], v, 1)
            buffer[72:75, :] = yflux[1, t, v, pl.ds(3 * x, 3), :]

            def at(by):
                return buffer[8 + by : 72 + by, :]

            y_term = 45.0 * (at(1) - at(-1)) - 9.0 * (at(2) - at(-2)) + (at(3) - at(-3))
            z_term = jnp.where(hit, replaced[t, v, x], along_z[v, :, cut])
            out_ref[v, 0, :, cut] = value - (y_term + z_term)


def advance(shocked, live_count, prepared, coefs):
    return pl.pallas_call(
        advance_body,
        grid=(CX,),
        out_shape=jax.ShapeDtypeStruct((VARIABLES, CX, CY, CZ), F32),
        in_specs=[SMEM, SMEM] + [VMEM] * 7,
        out_specs=pl.BlockSpec((VARIABLES, 1, CY, CZ), lambda x: (0, x, 0, 0)),
        scratch_shapes=[
            pltpu.VMEM((256, CZ), BF16),
            pltpu.VMEM((2, VARIABLES, CX, CY, 128), F32),
            pltpu.VMEM((ROWS, 128), F32),
            pltpu.VMEM((2, CY, 128), F32),
            pltpu.VMEM((2, 2, CY, 128), F32),
            pltpu.VMEM((VARIABLES, CY, 512), BF16),
            pltpu.VMEM((VARIABLES, CY, CZ), F32),
            pltpu.VMEM((2, 2, 80, 128), F32),
            pltpu.VMEM((VARIABLES, CZ, 128), F32),
            pltpu.VMEM((2, VARIABLES, PENCILS, 128), F32),
        ],
        compiler_params=pltpu.CompilerParams(vmem_limit_bytes=36 << 20),
        name="advance",
    )(shocked, live_count, *prepared, *coefs)


@functools.cache
def coefficients():
    weight = {1: 45.0, -1: -45.0, 2: -9.0, -2: 9.0, 3: 1.0, -3: -1.0}

    def coef(offset):
        return weight.get(offset, 0.0)

    zcoef = np.array([[coef(c - k) for k in range(CZ)] for c in range(CZ)])
    cells = [-3, -2, -1, CZ, CZ + 1, CZ + 2]
    hcoef = np.zeros((16, CZ))
    for j, c in enumerate(cells):
        for k in range(CZ):
            hcoef[j, k] = coef(c - k)
    return zcoef, hcoef


def on_device(conserved, char_left, char_right, shock_list, shock_count):
    shocked = shock_list.reshape(PENCILS)
    prepared = prepare(shocked, char_left, char_right, conserved)
    coefs = [jnp.asarray(m, BF16) for m in coefficients()]
    return advance(shocked, shock_count, prepared, coefs)


def solution(mesh):
    placed = (P(None, "gx", "gy", "gz"), P(), P(), P("gx", "gy", "gz", None), P("gx", "gy", "gz"))
    return jax.shard_map(
        on_device, mesh=mesh, in_specs=placed, out_specs=P(None, "gx", "gy", "gz"), check_vma=False
    )
```

```python
import functools

import jax
import jax.numpy as jnp
import numpy as np
from jax import lax
from jax.experimental import pallas as pl
from jax.experimental.pallas import tpu as pltpu
from jax.sharding import PartitionSpec as P

SPECIES = 9
VARIABLES = 14
CX, CY, CZ = 8, 64, 256
ROWS = CX * CY
PENCILS = 128
GROUP = 16
SIZE = VARIABLES * GROUP
CELLS = 280
TILES = 33
EPS = 0.5e-6
SCALE = 0.2 / 60.0

F32 = jnp.float32
BF16 = jnp.bfloat16
VMEM = pl.BlockSpec(memory_space=pltpu.VMEM)
SMEM = pl.BlockSpec(memory_space=pltpu.SMEM)
HBM = pl.BlockSpec(memory_space=pltpu.HBM)


def lanes(shape):
    return lax.broadcasted_iota(jnp.int32, shape, len(shape) - 1)


def split(values):
    high = values.astype(BF16)
    low = (values - high.astype(F32)).astype(BF16)
    return high, low


def dot(left, right):
    return jnp.dot(left, right, preferred_element_type=F32)


def state_of(read):
    density = read(0)
    for v in range(1, SPECIES):
        density = density + read(v)
    inverse = 1.0 / density
    m0, m1, m2 = read(9), read(10), read(11)
    squares = m0 * m0 + m1 * m1 + m2 * m2
    pressure = 0.4 * (read(12) - read(13) - 0.5 * squares * inverse)
    return m1 * inverse, m2 * inverse, pressure


def flux(value, velocity, pressure, scaled_pressure, v, normal):
    if v == SPECIES + 3:
        return (value + pressure) * velocity
    if v == SPECIES + normal:
        return value * velocity + scaled_pressure
    return value * velocity


def scaled(state):
    velocity1, velocity2, pressure = state
    return SCALE * velocity1, SCALE * velocity2, pressure, SCALE * pressure


def expand(matrix, scale, target):
    row = lax.broadcasted_iota(jnp.int32, (SIZE, SIZE), 0)
    column = lax.broadcasted_iota(jnp.int32, (SIZE, SIZE), 1)
    same = (row & (GROUP - 1)) == (column & (GROUP - 1))
    spread = (
        lax.broadcasted_iota(jnp.int32, (SIZE, VARIABLES), 0) // GROUP
        == lax.broadcasted_iota(jnp.int32, (SIZE, VARIABLES), 1)
    ).astype(BF16)
    gather = (
        lax.broadcasted_iota(jnp.int32, (VARIABLES, SIZE), 1) // GROUP
        == lax.broadcasted_iota(jnp.int32, (VARIABLES, SIZE), 0)
    ).astype(BF16)
    for part, places in zip(split(scale * matrix), ((0, 1), (2,))):
        wide = dot(spread, dot(part, gather).astype(BF16))
        wide = jnp.where(same, wide, 0.0).astype(BF16)
        for place in places:
            target[:, SIZE * place : SIZE * place + SIZE] = wide


def project(matrix, values):
    high, low = split(values)
    return dot(matrix[...], jnp.concatenate([high, low, high], axis=0))


def face_sums(speed, pull_ref, proj, velocity_ref, pressure_ref, scratch, sums):
    fast_ref, slow_ref, plus_ref, minus_ref, terms = scratch

    def sides(i, carry):
        rows = pl.ds(pl.multiple_of(8 * i, 8), 8)
        fast_ref[rows, :] = velocity_ref[rows, :] + speed
        slow_ref[rows, :] = velocity_ref[rows, :] - speed
        return carry

    lax.fori_loop(0, 34, sides, 0, unroll=2)

    def component(v, carry):
        pull = jnp.broadcast_to(pull_ref[0, pl.ds(v, 1), :], (8, 128))
        push = jnp.broadcast_to(pull_ref[1, pl.ds(v, 1), :], (8, 128))

        def fluxes(i, carry):
            rows = pl.ds(pl.multiple_of(8 * i, 8), 8)
            velocity = velocity_ref[rows, :]
            base = proj[v, rows, :]
            source = pressure_ref[rows, :] * (pull + velocity * push)
            plus_ref[rows, :] = fast_ref[rows, :] * base + source
            minus_ref[rows, :] = slow_ref[rows, :] * base + source
            return carry

        lax.fori_loop(0, 34, fluxes, 0, unroll=34)

        def pairs(i, carry):
            row = pl.multiple_of(8 * i, 8)
            for side, source in enumerate((plus_ref, minus_ref)):
                middle = source[pl.ds(row + 6, 8), :]
                x = middle - source[pl.ds(row + 5, 8), :]
                y = source[pl.ds(row + 7, 8), :] - middle
                xx, xy, yy = x * x, x * y, y * y
                shared = (xx + yy) * (2.0 / 3.0) + (EPS - xy * (11.0 / 6.0))
                lean, even, back = 1.0 / (shared + yy), 1.0 / (shared + xy), 1.0 / (shared + xx)
                x2, y2 = x + x, y + y
                if side == 0:
                    w0, w1, w2 = lean * lean, 6.0 * (even * even), 3.0 * (back * back)
                    n0, n1, n2 = 5.0 * y - x2, x + y2, (x2 + x2) - y
                else:
                    w0, w1, w2 = back * back, 6.0 * (even * even), 3.0 * (lean * lean)
                    n0, n1, n2 = 5.0 * x - y2, y + x2, (y2 + y2) - x
                for k, value in enumerate((w0, w1, w2, w0 * n0, w1 * n1, w2 * n2)):
                    terms[6 * side + k, pl.ds(row, 8), :] = value
            return carry

        lax.fori_loop(0, TILES, pairs, 0, unroll=33)

        def faces(i, carry):
            row = pl.multiple_of(8 * i, 8)

            def at(k, by):
                return terms[k, pl.ds(row + by, 8), :]

            gain = (at(3, 0) + at(4, 1) + at(5, 2)) / (at(0, 0) + at(1, 1) + at(2, 2))
            loss = (at(9, 3) + at(10, 2) + at(11, 1)) / (at(6, 3) + at(7, 2) + at(8, 1))
            base = plus_ref[pl.ds(row + 7, 8), :] + minus_ref[pl.ds(row + 8, 8), :]
            sums[v, pl.ds(row, 8), :] = base + (gain - loss) * (1.0 / 6.0)
            return carry

        lax.fori_loop(0, TILES, faces, 0, unroll=33)
        return carry

    lax.fori_loop(0, VARIABLES, component, 0)


def weno_terms(sums, kr_ref, across, terms_out):
    def chunk(i, carry):
        start = pl.multiple_of(32 * i, 8)

        def change(by):
            return sums[:, pl.ds(start + by + 1, 16), :] - sums[:, pl.ds(start + by, 16), :]

        values = jnp.concatenate([change(0), change(16)], axis=-1)
        result = project(kr_ref, values.reshape(SIZE, 256))
        for k in range(2):
            rows = pl.ds(pl.multiple_of(start + 16 * k, 8), 16)
            across[:, rows, :] = result[:, 128 * k : 128 * k + 128].reshape(VARIABLES, 16, 128)
        return carry

    lax.fori_loop(0, CZ // 32, chunk, 0, unroll=4)

    def turn_back(v, carry):
        for t in range(2):
            terms_out[t, v] = across[v, 128 * t : 128 * t + 128, :].T
        return carry

    lax.fori_loop(0, VARIABLES, turn_back, 0, unroll=2)


def prepare_body(
    list_ref, where_ref, left_ref, right_ref, u_hbm,
    u_ref, terms_out, yflux, zflux,
    sums, across, kr_out, proj, velocity_ref, pressure_ref, pull_ref,
    rows_ref, cells, kl_ref, up_send, down_send, z_send, y_recv, z_recv,
    load_sems, send_sems, recv_sems, *scratch,
):
    loads = []

    def load(index, t, x, y):
        copy = pltpu.make_async_copy(
            u_hbm.at[:, x, y, pl.ds(128 * t, 128)], u_ref.at[t, :, x, y], load_sems.at[index]
        )
        copy.start()
        loads.append(copy)

    every = pl.ds(0, CX)
    for t in range(2):
        load(len(loads), t, every, pl.ds(0, 8))
        load(len(loads), t, every, pl.ds(CY - 8, 8))
    gy, gz = lax.axis_index("gy"), lax.axis_index("gz")
    ny = lax.axis_size("gy")
    above, below = {"gy": lax.rem(gy + 1, ny)}, {"gy": lax.rem(gy + ny - 1, ny)}
    beside = {"gz": 1 - gz}
    barrier = pltpu.get_barrier_semaphore()
    for device in (above, below, beside):
        pl.semaphore_signal(barrier, inc=1, device_id=device, device_id_type=pl.DeviceIdType.MESH)

    def remote(index, source, target, device):
        return pltpu.make_async_remote_copy(
            src_ref=source,
            dst_ref=target,
            send_sem=send_sems.at[index],
            recv_sem=recv_sems.at[index],
            device_id=device,
            device_id_type=pl.DeviceIdType.MESH,
        )

    for x in range(2):
        for t in range(2):
            load(len(loads), t, pl.ds(x, 1), pl.ds(8, CY - 16))
    for copy in loads[:4]:
        copy.wait()
    for x in range(2, CX):
        for t in range(2):
            load(len(loads), t, pl.ds(x, 1), pl.ds(8, CY - 16))

    def y_ends(v, carry):
        for t in range(2):
            for x in range(CX):
                down_send[t, v, 3 * x : 3 * x + 3, :] = u_ref[t, v, x, 0:3, :]
                up_send[t, v, 3 * x : 3 * x + 3, :] = u_ref[t, v, x, CY - 3 : CY, :]
        return carry

    lax.fori_loop(0, VARIABLES, y_ends, 0)
    expand(left_ref[...], 0.5, kl_ref)
    for k in range(2):
        at = SPECIES + 2 + k
        pull_ref[k, 0:VARIABLES, :] = jnp.broadcast_to(
            0.5 * left_ref[:, at : at + 1], (VARIABLES, 128)
        )
    expand(right_ref[...], 0.2, kr_out)

    lane = lanes((CY, 128))
    source = lax.broadcasted_iota(jnp.int32, (CX * 128, 128), 0)
    place = lax.broadcasted_iota(jnp.int32, (CX * 128, 128), 1)
    within = ((source & 127) + 3) & 127
    wanted = jnp.minimum(place & 15, 5)
    select = ((place // 16 == source // 128) & (within == wanted)).astype(BF16)
    width = 128 * CX
    for part in range(2):
        some = range(part * CX // 2, (part + 1) * CX // 2)
        for copy in loads[4 + part * CX : 4 + (part + 1) * CX]:
            copy.wait()
        chosen = select[part * width // 2 : (part + 1) * width // 2]
        chosen = jnp.concatenate([chosen, chosen], axis=0)

        def z_ends(v, carry, part=part, some=some, chosen=chosen):
            highs, lows = [], []
            for x in some:
                high, low = split(jnp.where(lane < 64, u_ref[0, v, x], u_ref[1, v, x]))
                highs.append(high)
                lows.append(low)
            packed = dot(jnp.concatenate(highs + lows, axis=1), chosen)
            z_send[v] = packed if part == 0 else z_send[v] + packed
            return carry

        lax.fori_loop(0, VARIABLES, z_ends, 0, unroll=7)
        if part == 0:
            pl.semaphore_wait(barrier, 3)
            up = remote(0, up_send, y_recv.at[0], above)
            down = remote(1, down_send, y_recv.at[1], below)
            up.start()
            down.start()

    flat = u_ref.reshape(2, VARIABLES * ROWS, 128)
    packed = rows_ref.reshape(2, VARIABLES * PENCILS, 128)

    def gather(p, carry):
        row = list_ref[p]
        for t in range(2):
            for v in range(VARIABLES):
                packed[t, pl.ds(p + v * PENCILS, 1), :] = flat[t, pl.ds(row + v * ROWS, 1), :]
        return carry

    lax.fori_loop(0, 8, gather, 0, unroll=2)
    ends = remote(2, z_send, z_recv, beside)
    ends.start()
    lax.fori_loop(8, PENCILS, gather, 0, unroll=2)

    def turn(v, carry):
        for t in range(2):
            cells[v, 8 + 128 * t : 136 + 128 * t, :] = rows_ref[t, v].T
        return carry

    lax.fori_loop(0, VARIABLES, turn, 0, unroll=7)

    def wave(i, peak):
        rows = pl.ds(pl.multiple_of(8 * i, 8), 8)
        _, velocity, pressure = state_of(lambda v: cells[v, rows, :])
        velocity_ref[rows, :] = velocity
        pressure_ref[rows, :] = pressure
        return jnp.maximum(peak, jnp.abs(velocity))

    peak = lax.fori_loop(1, 33, wave, jnp.zeros((8, 128), F32), unroll=2)

    def chunk(i, carry):
        first = pl.ds(pl.multiple_of(32 * i + 8, 8), 16)
        second = pl.ds(pl.multiple_of(32 * i + 24, 8), 16)
        values = jnp.concatenate([cells[:, first, :], cells[:, second, :]], axis=-1)
        result = project(kl_ref, values.reshape(SIZE, 256))
        proj[:, first, :] = result[:, 0:128].reshape(VARIABLES, 16, 128)
        proj[:, second, :] = result[:, 128:256].reshape(VARIABLES, 16, 128)
        return carry

    lax.fori_loop(0, CZ // 32, chunk, 0, unroll=4)

    ends.wait()
    own_y = jnp.broadcast_to(where_ref[...] % CY, (2 * CY, PENCILS))
    pick = own_y == lax.broadcasted_iota(jnp.int32, (2 * CY, PENCILS), 0) % CY
    pick = pick.astype(BF16)
    own_x = jnp.broadcast_to(where_ref[...] // CY, (16, 128))

    def turn_ends(v, carry):
        values = z_recv[v]
        high = values.astype(BF16).astype(F32)
        both = jnp.concatenate([high, values - high], axis=0).T
        turned = dot(both.astype(BF16), pick)
        near = turned[0:16]
        for x in range(1, CX):
            near = jnp.where(own_x == x, turned[16 * x : 16 * x + 16], near)
        cells[v, 0:5, :] = near[0:5]
        cells[v, 5:8, :] = near[0:3]
        cells[v, 264:267, :] = near[3:6]
        cells[v, 267:272, :] = near[0:5]
        return carry

    lax.fori_loop(0, VARIABLES, turn_ends, 0, unroll=7)
    peak = wave(0, peak)
    peak = wave(33, peak)
    speed = jnp.broadcast_to(jnp.max(peak, axis=0, keepdims=True) + 1.0, (8, 128))
    values = jnp.concatenate([cells[:, 0:8, :], cells[:, 264:272, :]], axis=1)
    result = project(kl_ref, values.reshape(SIZE, 128)).reshape(VARIABLES, 16, 128)
    proj[:, 0:8, :] = result[:, 0:8]
    proj[:, 264:272, :] = result[:, 8:16]

    _, velocity, pressure, scaled_pressure = scaled(state_of(lambda v: z_recv[v]))
    for v in range(VARIABLES):
        high, low = split(flux(z_recv[v], velocity, pressure, scaled_pressure, v, 2))
        zflux[v, :, 0:128] = high
        zflux[v, :, 128:256] = low

    face_sums(speed, pull_ref, proj, velocity_ref, pressure_ref, scratch, sums)
    weno_terms(sums, kr_out, across, terms_out)

    up.wait()
    down.wait()
    for side in range(2):
        for t in range(2):
            state = scaled(state_of(lambda v: y_recv[side, t, v]))
            for v in range(VARIABLES):
                yflux[side, t, v] = flux(y_recv[side, t, v], state[0], state[2], state[3], v, 1)


def prepare(shocked, left, right, conserved):
    return pl.pallas_call(
        prepare_body,
        out_shape=(
            pltpu.VMEM((2, VARIABLES, CX, CY, 128), F32),
            pltpu.VMEM((2, VARIABLES, PENCILS, 128), F32),
            pltpu.VMEM((2, 2, VARIABLES, 3 * CX, 128), F32),
            pltpu.VMEM((VARIABLES, CY, 256), BF16),
        ),
        in_specs=[SMEM, VMEM, VMEM, VMEM, HBM],
        out_specs=(VMEM,) * 4,
        scratch_shapes=[
            pltpu.VMEM((VARIABLES, CELLS, 128), F32),
            pltpu.VMEM((VARIABLES, CZ, 128), F32),
            pltpu.VMEM((SIZE, 3 * SIZE), BF16),
            pltpu.VMEM((VARIABLES, CELLS, 128), F32),
            pltpu.VMEM((CELLS, 128), F32),
            pltpu.VMEM((CELLS, 128), F32),
            pltpu.VMEM((2, 16, 128), F32),
            pltpu.VMEM((2, VARIABLES, PENCILS, 128), F32),
            pltpu.VMEM((VARIABLES, 272, 128), F32),
            pltpu.VMEM((SIZE, 3 * SIZE), BF16),
            pltpu.VMEM((2, VARIABLES, 3 * CX, 128), F32),
            pltpu.VMEM((2, VARIABLES, 3 * CX, 128), F32),
            pltpu.VMEM((VARIABLES, CY, 128), F32),
            pltpu.VMEM((2, 2, VARIABLES, 3 * CX, 128), F32),
            pltpu.VMEM((VARIABLES, CY, 128), F32),
            pltpu.SemaphoreType.DMA((4 + 2 * CX,)),
            pltpu.SemaphoreType.DMA((3,)),
            pltpu.SemaphoreType.DMA((3,)),
            pltpu.VMEM((CELLS, 128), F32),
            pltpu.VMEM((CELLS, 128), F32),
            pltpu.VMEM((CELLS, 128), F32),
            pltpu.VMEM((CELLS, 128), F32),
            pltpu.VMEM((12, CELLS, 128), F32),
        ],
        compiler_params=pltpu.CompilerParams(
            collective_id=0, has_side_effects=True, vmem_limit_bytes=46 << 20
        ),
        name="prepare",
    )(shocked, shocked.reshape(1, PENCILS), left, right, conserved)


def advance_body(
    list_ref, count_ref, u_ref,
    terms_ref, yflux, zflux, zcoef_ref, hcoef_ref,
    out_ref,
    hx_ref, replaced, mask_ref, v1_ref, p_ref, stage, along_z, along_y,
):
    x = pl.program_id(0)

    @pl.when(x == 0)
    def _():
        hx_ref[...] = jnp.zeros((256, CZ), BF16)
        mask_ref[...] = jnp.zeros((ROWS, 128), F32)
        flat = replaced.reshape(2, VARIABLES * ROWS, 128)
        packed = terms_ref.reshape(2, VARIABLES * PENCILS, 128)

        def scatter(p, carry):
            row = list_ref[p]
            mask_ref[pl.ds(row, 1), :] = jnp.ones((1, 128), F32)
            for t in range(2):
                for v in range(VARIABLES):
                    flat[t, pl.ds(row + v * ROWS, 1), :] = packed[t, pl.ds(p + v * PENCILS, 1), :]
            return carry

        lax.fori_loop(0, count_ref[0, 0, 0], scatter, 0)

    @pl.when(x > 0)
    def _():
        for part in range(2):
            old = pl.ds(pl.multiple_of(128 * part + 16 * x - 16, 16), 16)
            hx_ref[old, :] = jnp.zeros((16, CZ), BF16)

    for part in range(2):
        new = pl.ds(pl.multiple_of(128 * part + 16 * x, 16), 16)
        hx_ref[new, :] = hcoef_ref[...]

    for t in range(2):
        cut = slice(128 * t, 128 * t + 128)
        velocity1, velocity2, pressure, scaled_pressure = scaled(
            state_of(lambda v: u_ref[t, v, x])
        )
        v1_ref[t] = velocity1
        p_ref[0, t] = pressure
        p_ref[1, t] = scaled_pressure
        for v in range(VARIABLES):
            high, low = split(flux(u_ref[t, v, x], velocity2, pressure, scaled_pressure, v, 2))
            stage[v, :, cut] = high
            stage[v, :, 256 + 128 * t : 384 + 128 * t] = low

    rows = VARIABLES * CY
    along_z[...] = dot(
        jnp.concatenate([stage[...].reshape(rows, 512), zflux[...].reshape(rows, 256)], axis=1),
        jnp.concatenate([zcoef_ref[...], zcoef_ref[...], hx_ref[...]], axis=0),
    ).reshape(VARIABLES, CY, CZ)

    hit = mask_ref[pl.ds(pl.multiple_of(CY * x, CY), CY), :] > 0.5
    for v in range(VARIABLES):
        for t in range(2):
            cut = slice(128 * t, 128 * t + 128)
            buffer = along_y.at[v % 2, t]
            value = u_ref[t, v, x]
            buffer[5:8, :] = yflux[0, t, v, pl.ds(3 * x, 3), :]
            buffer[8:72, :] = flux(value, v1_ref[t], p_ref[0, t], p_ref[1, t], v, 1)
            buffer[72:75, :] = yflux[1, t, v, pl.ds(3 * x, 3), :]

            def at(by):
                return buffer[8 + by : 72 + by, :]

            y_term = 45.0 * (at(1) - at(-1)) - 9.0 * (at(2) - at(-2)) + (at(3) - at(-3))
            z_term = jnp.where(hit, replaced[t, v, x], along_z[v, :, cut])
            out_ref[v, 0, :, cut] = value - (y_term + z_term)


def advance(shocked, live_count, prepared, coefs):
    return pl.pallas_call(
        advance_body,
        grid=(CX,),
        out_shape=jax.ShapeDtypeStruct((VARIABLES, CX, CY, CZ), F32),
        in_specs=[SMEM, SMEM] + [VMEM] * 6,
        out_specs=pl.BlockSpec((VARIABLES, 1, CY, CZ), lambda x: (0, x, 0, 0)),
        scratch_shapes=[
            pltpu.VMEM((256, CZ), BF16),
            pltpu.VMEM((2, VARIABLES, CX, CY, 128), F32),
            pltpu.VMEM((ROWS, 128), F32),
            pltpu.VMEM((2, CY, 128), F32),
            pltpu.VMEM((2, 2, CY, 128), F32),
            pltpu.VMEM((VARIABLES, CY, 512), BF16),
            pltpu.VMEM((VARIABLES, CY, CZ), F32),
            pltpu.VMEM((2, 2, 80, 128), F32),
        ],
        compiler_params=pltpu.CompilerParams(vmem_limit_bytes=36 << 20),
        name="advance",
    )(shocked, live_count, *prepared, *coefs)


@functools.cache
def coefficients():
    weight = {1: 45.0, -1: -45.0, 2: -9.0, -2: 9.0, 3: 1.0, -3: -1.0}

    def coef(offset):
        return weight.get(offset, 0.0)

    zcoef = np.array([[coef(c - k) for k in range(CZ)] for c in range(CZ)])
    cells = [-3, -2, -1, CZ, CZ + 1, CZ + 2]
    hcoef = np.zeros((16, CZ))
    for j, c in enumerate(cells):
        for k in range(CZ):
            hcoef[j, k] = coef(c - k)
    return zcoef, hcoef


def on_device(conserved, char_left, char_right, shock_list, shock_count):
    shocked = shock_list.reshape(PENCILS)
    prepared = prepare(shocked, char_left, char_right, conserved)
    coefs = [jnp.asarray(m, BF16) for m in coefficients()]
    return advance(shocked, shock_count, prepared, coefs)


def solution(mesh):
    placed = (P(None, "gx", "gy", "gz"), P(), P(), P("gx", "gy", "gz", None), P("gx", "gy", "gz"))
    return jax.shard_map(
        on_device, mesh=mesh, in_specs=placed, out_specs=P(None, "gx", "gy", "gz"), check_vma=False
    )
```

```python
import functools

import jax
import jax.numpy as jnp
import numpy as np
from jax import lax
from jax.experimental import pallas as pl
from jax.experimental.pallas import tpu as pltpu
from jax.sharding import PartitionSpec as P

SPECIES = 9
VARIABLES = 14
CX, CY, CZ = 8, 64, 256
ROWS = CX * CY
PENCILS = 128
GROUP = 16
SIZE = VARIABLES * GROUP
CELLS = 280
TILES = 33
EPS = 0.5e-6
SCALE = 0.2 / 60.0

F32 = jnp.float32
BF16 = jnp.bfloat16
VMEM = pl.BlockSpec(memory_space=pltpu.VMEM)
SMEM = pl.BlockSpec(memory_space=pltpu.SMEM)
HBM = pl.BlockSpec(memory_space=pltpu.HBM)


def lanes(shape):
    return lax.broadcasted_iota(jnp.int32, shape, len(shape) - 1)


def split(values):
    high = values.astype(BF16)
    low = (values - high.astype(F32)).astype(BF16)
    return high, low


def dot(left, right):
    return jnp.dot(left, right, preferred_element_type=F32)


def state_of(read):
    density = read(0)
    for v in range(1, SPECIES):
        density = density + read(v)
    inverse = 1.0 / density
    m0, m1, m2 = read(9), read(10), read(11)
    squares = m0 * m0 + m1 * m1 + m2 * m2
    pressure = 0.4 * (read(12) - read(13) - 0.5 * squares * inverse)
    return m1 * inverse, m2 * inverse, pressure


def flux(value, velocity, pressure, scaled_pressure, v, normal):
    if v == SPECIES + 3:
        return (value + pressure) * velocity
    if v == SPECIES + normal:
        return value * velocity + scaled_pressure
    return value * velocity


def scaled(state):
    velocity1, velocity2, pressure = state
    return SCALE * velocity1, SCALE * velocity2, pressure, SCALE * pressure


def expand(matrix, scale, target):
    row = lax.broadcasted_iota(jnp.int32, (SIZE, SIZE), 0)
    column = lax.broadcasted_iota(jnp.int32, (SIZE, SIZE), 1)
    same = (row & (GROUP - 1)) == (column & (GROUP - 1))
    spread = (
        lax.broadcasted_iota(jnp.int32, (SIZE, VARIABLES), 0) // GROUP
        == lax.broadcasted_iota(jnp.int32, (SIZE, VARIABLES), 1)
    ).astype(BF16)
    gather = (
        lax.broadcasted_iota(jnp.int32, (VARIABLES, SIZE), 1) // GROUP
        == lax.broadcasted_iota(jnp.int32, (VARIABLES, SIZE), 0)
    ).astype(BF16)
    for part, places in zip(split(scale * matrix), ((0, 1), (2,))):
        wide = dot(spread, dot(part, gather).astype(BF16))
        wide = jnp.where(same, wide, 0.0).astype(BF16)
        for place in places:
            target[:, SIZE * place : SIZE * place + SIZE] = wide


def project(matrix, values):
    high, low = split(values)
    return dot(matrix[...], jnp.concatenate([high, low, high], axis=0))


def face_sums(speed, pull_ref, proj, velocity_ref, pressure_ref, scratch, sums):
    fast_ref, slow_ref, plus_ref, minus_ref, terms = scratch

    def sides(i, carry):
        rows = pl.ds(pl.multiple_of(8 * i, 8), 8)
        fast_ref[rows, :] = velocity_ref[rows, :] + speed
        slow_ref[rows, :] = velocity_ref[rows, :] - speed
        return carry

    lax.fori_loop(0, 34, sides, 0, unroll=2)

    def component(v, carry):
        pull = jnp.broadcast_to(pull_ref[0, pl.ds(v, 1), :], (8, 128))
        push = jnp.broadcast_to(pull_ref[1, pl.ds(v, 1), :], (8, 128))

        def fluxes(i, carry):
            rows = pl.ds(pl.multiple_of(8 * i, 8), 8)
            velocity = velocity_ref[rows, :]
            base = proj[v, rows, :]
            source = pressure_ref[rows, :] * (pull + velocity * push)
            plus_ref[rows, :] = fast_ref[rows, :] * base + source
            minus_ref[rows, :] = slow_ref[rows, :] * base + source
            return carry

        lax.fori_loop(0, 34, fluxes, 0, unroll=34)

        def pairs(i, carry):
            row = pl.multiple_of(8 * i, 8)
            for side, source in enumerate((plus_ref, minus_ref)):
                middle = source[pl.ds(row + 6, 8), :]
                x = middle - source[pl.ds(row + 5, 8), :]
                y = source[pl.ds(row + 7, 8), :] - middle
                xx, xy, yy = x * x, x * y, y * y
                shared = (xx + yy) * (2.0 / 3.0) + (EPS - xy * (11.0 / 6.0))
                lean, even, back = 1.0 / (shared + yy), 1.0 / (shared + xy), 1.0 / (shared + xx)
                x2, y2 = x + x, y + y
                if side == 0:
                    w0, w1, w2 = lean * lean, 6.0 * (even * even), 3.0 * (back * back)
                    n0, n1, n2 = 5.0 * y - x2, x + y2, (x2 + x2) - y
                else:
                    w0, w1, w2 = back * back, 6.0 * (even * even), 3.0 * (lean * lean)
                    n0, n1, n2 = 5.0 * x - y2, y + x2, (y2 + y2) - x
                for k, value in enumerate((w0, w1, w2, w0 * n0, w1 * n1, w2 * n2)):
                    terms[6 * side + k, pl.ds(row, 8), :] = value
            return carry

        lax.fori_loop(0, TILES, pairs, 0, unroll=33)

        def faces(i, carry):
            row = pl.multiple_of(8 * i, 8)

            def at(k, by):
                return terms[k, pl.ds(row + by, 8), :]

            gain = (at(3, 0) + at(4, 1) + at(5, 2)) / (at(0, 0) + at(1, 1) + at(2, 2))
            loss = (at(9, 3) + at(10, 2) + at(11, 1)) / (at(6, 3) + at(7, 2) + at(8, 1))
            base = plus_ref[pl.ds(row + 7, 8), :] + minus_ref[pl.ds(row + 8, 8), :]
            sums[v, pl.ds(row, 8), :] = base + (gain - loss) * (1.0 / 6.0)
            return carry

        lax.fori_loop(0, TILES, faces, 0, unroll=33)
        return carry

    lax.fori_loop(0, VARIABLES, component, 0)


def weno_terms(sums, kr_ref, across, terms_out):
    def chunk(i, carry):
        start = pl.multiple_of(32 * i, 8)

        def change(by):
            return sums[:, pl.ds(start + by + 1, 16), :] - sums[:, pl.ds(start + by, 16), :]

        values = jnp.concatenate([change(0), change(16)], axis=-1)
        result = project(kr_ref, values.reshape(SIZE, 256))
        for k in range(2):
            rows = pl.ds(pl.multiple_of(start + 16 * k, 8), 16)
            across[:, rows, :] = result[:, 128 * k : 128 * k + 128].reshape(VARIABLES, 16, 128)
        return carry

    lax.fori_loop(0, CZ // 32, chunk, 0, unroll=8)

    def turn_back(v, carry):
        for t in range(2):
            terms_out[t, v] = across[v, 128 * t : 128 * t + 128, :].T
        return carry

    lax.fori_loop(0, VARIABLES, turn_back, 0, unroll=7)


def prepare_body(
    list_ref, where_ref, left_ref, right_ref, u_hbm,
    u_ref, terms_out, yflux, zflux,
    sums, across, kr_out, proj, velocity_ref, pressure_ref, pull_ref,
    rows_ref, cells, kl_ref, up_send, down_send, z_send, y_recv, z_recv,
    load_sems, send_sems, recv_sems, *scratch,
):
    loads = []

    def load(index, t, x, y):
        copy = pltpu.make_async_copy(
            u_hbm.at[:, x, y, pl.ds(128 * t, 128)], u_ref.at[t, :, x, y], load_sems.at[index]
        )
        copy.start()
        loads.append(copy)

    every = pl.ds(0, CX)
    for t in range(2):
        load(len(loads), t, every, pl.ds(0, 8))
        load(len(loads), t, every, pl.ds(CY - 8, 8))
    gy, gz = lax.axis_index("gy"), lax.axis_index("gz")
    ny = lax.axis_size("gy")
    above, below = {"gy": lax.rem(gy + 1, ny)}, {"gy": lax.rem(gy + ny - 1, ny)}
    beside = {"gz": 1 - gz}
    barrier = pltpu.get_barrier_semaphore()
    for device in (above, below, beside):
        pl.semaphore_signal(barrier, inc=1, device_id=device, device_id_type=pl.DeviceIdType.MESH)

    def remote(index, source, target, device):
        return pltpu.make_async_remote_copy(
            src_ref=source,
            dst_ref=target,
            send_sem=send_sems.at[index],
            recv_sem=recv_sems.at[index],
            device_id=device,
            device_id_type=pl.DeviceIdType.MESH,
        )

    for x in range(2):
        for t in range(2):
            load(len(loads), t, pl.ds(x, 1), pl.ds(8, CY - 16))
    for copy in loads[:4]:
        copy.wait()
    for x in range(2, CX):
        for t in range(2):
            load(len(loads), t, pl.ds(x, 1), pl.ds(8, CY - 16))

    def y_ends(v, carry):
        for t in range(2):
            for x in range(CX):
                down_send[t, v, 3 * x : 3 * x + 3, :] = u_ref[t, v, x, 0:3, :]
                up_send[t, v, 3 * x : 3 * x + 3, :] = u_ref[t, v, x, CY - 3 : CY, :]
        return carry

    lax.fori_loop(0, VARIABLES, y_ends, 0)
    expand(left_ref[...], 0.5, kl_ref)
    for k in range(2):
        at = SPECIES + 2 + k
        pull_ref[k, 0:VARIABLES, :] = jnp.broadcast_to(
            0.5 * left_ref[:, at : at + 1], (VARIABLES, 128)
        )
    expand(right_ref[...], 0.2, kr_out)

    lane = lanes((CY, 128))
    source = lax.broadcasted_iota(jnp.int32, (CX * 128, 128), 0)
    place = lax.broadcasted_iota(jnp.int32, (CX * 128, 128), 1)
    within = ((source & 127) + 3) & 127
    wanted = jnp.minimum(place & 15, 5)
    select = ((place // 16 == source // 128) & (within == wanted)).astype(BF16)
    width = 128 * CX
    for part in range(2):
        some = range(part * CX // 2, (part + 1) * CX // 2)
        for copy in loads[4 + part * CX : 4 + (part + 1) * CX]:
            copy.wait()
        chosen = select[part * width // 2 : (part + 1) * width // 2]
        chosen = jnp.concatenate([chosen, chosen], axis=0)

        def z_ends(v, carry, part=part, some=some, chosen=chosen):
            highs, lows = [], []
            for x in some:
                high, low = split(jnp.where(lane < 64, u_ref[0, v, x], u_ref[1, v, x]))
                highs.append(high)
                lows.append(low)
            packed = dot(jnp.concatenate(highs + lows, axis=1), chosen)
            z_send[v] = packed if part == 0 else z_send[v] + packed
            return carry

        lax.fori_loop(0, VARIABLES, z_ends, 0, unroll=7)
        if part == 0:
            pl.semaphore_wait(barrier, 3)
            up = remote(0, up_send, y_recv.at[0], above)
            down = remote(1, down_send, y_recv.at[1], below)
            up.start()
            down.start()

    flat = u_ref.reshape(2, VARIABLES * ROWS, 128)
    packed = rows_ref.reshape(2, VARIABLES * PENCILS, 128)

    def gather(p, carry):
        row = list_ref[p]
        for t in range(2):
            for v in range(VARIABLES):
                packed[t, pl.ds(p + v * PENCILS, 1), :] = flat[t, pl.ds(row + v * ROWS, 1), :]
        return carry

    lax.fori_loop(0, 8, gather, 0, unroll=2)
    ends = remote(2, z_send, z_recv, beside)
    ends.start()
    lax.fori_loop(8, PENCILS, gather, 0, unroll=2)

    def turn(v, carry):
        for t in range(2):
            cells[v, 8 + 128 * t : 136 + 128 * t, :] = rows_ref[t, v].T
        return carry

    lax.fori_loop(0, VARIABLES, turn, 0, unroll=7)

    def wave(i, peak):
        rows = pl.ds(pl.multiple_of(8 * i, 8), 8)
        _, velocity, pressure = state_of(lambda v: cells[v, rows, :])
        velocity_ref[rows, :] = velocity
        pressure_ref[rows, :] = pressure
        return jnp.maximum(peak, jnp.abs(velocity))

    peak = lax.fori_loop(1, 33, wave, jnp.zeros((8, 128), F32), unroll=4)

    def chunk(i, carry):
        first = pl.ds(pl.multiple_of(32 * i + 8, 8), 16)
        second = pl.ds(pl.multiple_of(32 * i + 24, 8), 16)
        values = jnp.concatenate([cells[:, first, :], cells[:, second, :]], axis=-1)
        result = project(kl_ref, values.reshape(SIZE, 256))
        proj[:, first, :] = result[:, 0:128].reshape(VARIABLES, 16, 128)
        proj[:, second, :] = result[:, 128:256].reshape(VARIABLES, 16, 128)
        return carry

    lax.fori_loop(0, CZ // 32, chunk, 0, unroll=8)

    ends.wait()
    own_y = jnp.broadcast_to(where_ref[...] % CY, (2 * CY, PENCILS))
    pick = own_y == lax.broadcasted_iota(jnp.int32, (2 * CY, PENCILS), 0) % CY
    pick = pick.astype(BF16)
    own_x = jnp.broadcast_to(where_ref[...] // CY, (16, 128))

    def turn_ends(v, carry):
        values = z_recv[v]
        high = values.astype(BF16).astype(F32)
        both = jnp.concatenate([high, values - high], axis=0).T
        turned = dot(both.astype(BF16), pick)
        near = turned[0:16]
        for x in range(1, CX):
            near = jnp.where(own_x == x, turned[16 * x : 16 * x + 16], near)
        cells[v, 0:5, :] = near[0:5]
        cells[v, 5:8, :] = near[0:3]
        cells[v, 264:267, :] = near[3:6]
        cells[v, 267:272, :] = near[0:5]
        return carry

    lax.fori_loop(0, VARIABLES, turn_ends, 0, unroll=7)
    peak = wave(0, peak)
    peak = wave(33, peak)
    speed = jnp.broadcast_to(jnp.max(peak, axis=0, keepdims=True) + 1.0, (8, 128))
    values = jnp.concatenate([cells[:, 0:8, :], cells[:, 264:272, :]], axis=1)
    result = project(kl_ref, values.reshape(SIZE, 128)).reshape(VARIABLES, 16, 128)
    proj[:, 0:8, :] = result[:, 0:8]
    proj[:, 264:272, :] = result[:, 8:16]

    _, velocity, pressure, scaled_pressure = scaled(state_of(lambda v: z_recv[v]))
    for v in range(VARIABLES):
        high, low = split(flux(z_recv[v], velocity, pressure, scaled_pressure, v, 2))
        zflux[v, :, 0:128] = high
        zflux[v, :, 128:256] = low

    face_sums(speed, pull_ref, proj, velocity_ref, pressure_ref, scratch, sums)
    weno_terms(sums, kr_out, across, terms_out)

    up.wait()
    down.wait()
    for side in range(2):
        for t in range(2):
            state = scaled(state_of(lambda v: y_recv[side, t, v]))
            for v in range(VARIABLES):
                yflux[side, t, v] = flux(y_recv[side, t, v], state[0], state[2], state[3], v, 1)


def prepare(shocked, left, right, conserved):
    return pl.pallas_call(
        prepare_body,
        out_shape=(
            pltpu.VMEM((2, VARIABLES, CX, CY, 128), F32),
            pltpu.VMEM((2, VARIABLES, PENCILS, 128), F32),
            pltpu.VMEM((2, 2, VARIABLES, 3 * CX, 128), F32),
            pltpu.VMEM((VARIABLES, CY, 256), BF16),
        ),
        in_specs=[SMEM, VMEM, VMEM, VMEM, HBM],
        out_specs=(VMEM,) * 4,
        scratch_shapes=[
            pltpu.VMEM((VARIABLES, CELLS, 128), F32),
            pltpu.VMEM((VARIABLES, CZ, 128), F32),
            pltpu.VMEM((SIZE, 3 * SIZE), BF16),
            pltpu.VMEM((VARIABLES, CELLS, 128), F32),
            pltpu.VMEM((CELLS, 128), F32),
            pltpu.VMEM((CELLS, 128), F32),
            pltpu.VMEM((2, 16, 128), F32),
            pltpu.VMEM((2, VARIABLES, PENCILS, 128), F32),
            pltpu.VMEM((VARIABLES, 272, 128), F32),
            pltpu.VMEM((SIZE, 3 * SIZE), BF16),
            pltpu.VMEM((2, VARIABLES, 3 * CX, 128), F32),
            pltpu.VMEM((2, VARIABLES, 3 * CX, 128), F32),
            pltpu.VMEM((VARIABLES, CY, 128), F32),
            pltpu.VMEM((2, 2, VARIABLES, 3 * CX, 128), F32),
            pltpu.VMEM((VARIABLES, CY, 128), F32),
            pltpu.SemaphoreType.DMA((4 + 2 * CX,)),
            pltpu.SemaphoreType.DMA((3,)),
            pltpu.SemaphoreType.DMA((3,)),
            pltpu.VMEM((CELLS, 128), F32),
            pltpu.VMEM((CELLS, 128), F32),
            pltpu.VMEM((CELLS, 128), F32),
            pltpu.VMEM((CELLS, 128), F32),
            pltpu.VMEM((12, CELLS, 128), F32),
        ],
        compiler_params=pltpu.CompilerParams(
            collective_id=0, has_side_effects=True, vmem_limit_bytes=46 << 20
        ),
        name="prepare",
    )(shocked, shocked.reshape(1, PENCILS), left, right, conserved)


def advance_body(
    list_ref, count_ref, u_ref,
    terms_ref, yflux, zflux, zcoef_ref, hcoef_ref,
    out_ref,
    hx_ref, replaced, mask_ref, v1_ref, p_ref, stage, along_z, along_y,
):
    x = pl.program_id(0)

    @pl.when(x == 0)
    def _():
        hx_ref[...] = jnp.zeros((256, CZ), BF16)
        mask_ref[...] = jnp.zeros((ROWS, 128), F32)
        flat = replaced.reshape(2, VARIABLES * ROWS, 128)
        packed = terms_ref.reshape(2, VARIABLES * PENCILS, 128)

        def scatter(p, carry):
            row = list_ref[p]
            mask_ref[pl.ds(row, 1), :] = jnp.ones((1, 128), F32)
            for t in range(2):
                for v in range(VARIABLES):
                    flat[t, pl.ds(row + v * ROWS, 1), :] = packed[t, pl.ds(p + v * PENCILS, 1), :]
            return carry

        lax.fori_loop(0, count_ref[0, 0, 0], scatter, 0)

    @pl.when(x > 0)
    def _():
        for part in range(2):
            old = pl.ds(pl.multiple_of(128 * part + 16 * x - 16, 16), 16)
            hx_ref[old, :] = jnp.zeros((16, CZ), BF16)

    for part in range(2):
        new = pl.ds(pl.multiple_of(128 * part + 16 * x, 16), 16)
        hx_ref[new, :] = hcoef_ref[...]

    for t in range(2):
        cut = slice(128 * t, 128 * t + 128)
        velocity1, velocity2, pressure, scaled_pressure = scaled(
            state_of(lambda v: u_ref[t, v, x])
        )
        v1_ref[t] = velocity1
        p_ref[0, t] = pressure
        p_ref[1, t] = scaled_pressure
        for v in range(VARIABLES):
            high, low = split(flux(u_ref[t, v, x], velocity2, pressure, scaled_pressure, v, 2))
            stage[v, :, cut] = high
            stage[v, :, 256 + 128 * t : 384 + 128 * t] = low

    rows = VARIABLES * CY
    along_z[...] = dot(
        jnp.concatenate([stage[...].reshape(rows, 512), zflux[...].reshape(rows, 256)], axis=1),
        jnp.concatenate([zcoef_ref[...], zcoef_ref[...], hx_ref[...]], axis=0),
    ).reshape(VARIABLES, CY, CZ)

    hit = mask_ref[pl.ds(pl.multiple_of(CY * x, CY), CY), :] > 0.5
    for v in range(VARIABLES):
        for t in range(2):
            cut = slice(128 * t, 128 * t + 128)
            buffer = along_y.at[v % 2, t]
            value = u_ref[t, v, x]
            buffer[5:8, :] = yflux[0, t, v, pl.ds(3 * x, 3), :]
            buffer[8:72, :] = flux(value, v1_ref[t], p_ref[0, t], p_ref[1, t], v, 1)
            buffer[72:75, :] = yflux[1, t, v, pl.ds(3 * x, 3), :]

            def at(by):
                return buffer[8 + by : 72 + by, :]

            y_term = 45.0 * (at(1) - at(-1)) - 9.0 * (at(2) - at(-2)) + (at(3) - at(-3))
            z_term = jnp.where(hit, replaced[t, v, x], along_z[v, :, cut])
            out_ref[v, 0, :, cut] = value - (y_term + z_term)


def advance(shocked, live_count, prepared, coefs):
    return pl.pallas_call(
        advance_body,
        grid=(CX,),
        out_shape=jax.ShapeDtypeStruct((VARIABLES, CX, CY, CZ), F32),
        in_specs=[SMEM, SMEM] + [VMEM] * 6,
        out_specs=pl.BlockSpec((VARIABLES, 1, CY, CZ), lambda x: (0, x, 0, 0)),
        scratch_shapes=[
            pltpu.VMEM((256, CZ), BF16),
            pltpu.VMEM((2, VARIABLES, CX, CY, 128), F32),
            pltpu.VMEM((ROWS, 128), F32),
            pltpu.VMEM((2, CY, 128), F32),
            pltpu.VMEM((2, 2, CY, 128), F32),
            pltpu.VMEM((VARIABLES, CY, 512), BF16),
            pltpu.VMEM((VARIABLES, CY, CZ), F32),
            pltpu.VMEM((2, 2, 80, 128), F32),
        ],
        compiler_params=pltpu.CompilerParams(vmem_limit_bytes=36 << 20),
        name="advance",
    )(shocked, live_count, *prepared, *coefs)


@functools.cache
def coefficients():
    weight = {1: 45.0, -1: -45.0, 2: -9.0, -2: 9.0, 3: 1.0, -3: -1.0}

    def coef(offset):
        return weight.get(offset, 0.0)

    zcoef = np.array([[coef(c - k) for k in range(CZ)] for c in range(CZ)])
    cells = [-3, -2, -1, CZ, CZ + 1, CZ + 2]
    hcoef = np.zeros((16, CZ))
    for j, c in enumerate(cells):
        for k in range(CZ):
            hcoef[j, k] = coef(c - k)
    return zcoef, hcoef


def on_device(conserved, char_left, char_right, shock_list, shock_count):
    shocked = shock_list.reshape(PENCILS)
    prepared = prepare(shocked, char_left, char_right, conserved)
    coefs = [jnp.asarray(m, BF16) for m in coefficients()]
    return advance(shocked, shock_count, prepared, coefs)


def solution(mesh):
    placed = (P(None, "gx", "gy", "gz"), P(), P(), P("gx", "gy", "gz", None), P("gx", "gy", "gz"))
    return jax.shard_map(
        on_device, mesh=mesh, in_specs=placed, out_specs=P(None, "gx", "gy", "gz"), check_vma=False
    )
```
